32 devices in a mesh: ctx: 8 (over z, x), tp: 4 (over y, core).
Axes of the slice: x: 2, y: 2, z: 4, core: 2. Of those that a mesh axis runs over, the one named last changes fastest.
Arguments:
- queries: bfloat16 [2048, 8192], P('ctx', 'tp'), may hold values from -12 to 12
- keys: bfloat16 [2048, 1024], P('ctx', 'tp'), may hold values from -12 to 12
- values: bfloat16 [2048, 1024], P('ctx', 'tp'), may hold values from -6 to 6
- lengths: int32 [4], replicated, may hold values from 1 to 1536, 2048 in all
- out_weight: bfloat16 [8192, 4096], P('tp'), may hold values from -0.59765625 to 0.59765625
Outputs:
- mixed: bfloat16 [2048, 4096], P('ctx', 'tp')
The draws below stay inside these ranges and needn't reach their ends.
Inputs may be any that keep to these rules, and one draw needn't show every extreme that they name: The 4 lengths sum to 2048; the longest is exactly 1536.
All inputs are finite; a program needn't handle non-finite values.
Results may differ from the reference program's by a relative error of at most 0.014.
Values may be sent and summed in bfloat16 or wider, within the bound.
A program may use at most 192 MiB of HBM per device.

```python
import math
import jax
import jax.numpy as jnp
import numpy as np
from jax import lax

QH = 64
KVH = 8
HD = 128
FEAT = 4096
TOK_DEV = 256
DOCS = 4
MOST = 1536
PACKED_TOKENS = 2048
N_CTX = 8
N_TP = 4


def paired_draw(key):
    root_random_key = jax.random.fold_in(key, 7)
    random_key_for_query, random_key_for_keys = jax.random.split(root_random_key, 2)
    query_draw = jax.random.truncated_normal(random_key_for_query, -4.0, 4.0, (PACKED_TOKENS, QH * HD), jnp.float32)
    sampled_keys = jax.random.truncated_normal(random_key_for_keys, -4.0, 4.0, (PACKED_TOKENS, KVH * HD), jnp.float32)
    return (query_draw, sampled_keys)


def draw_queries(key, part):
    return paired_draw(key)[0].astype(jnp.bfloat16)


def draw_keys(key, part):
    return paired_draw(key)[1].astype(jnp.bfloat16)


def block_levels(key, shape, shards, least, high):
    loudness, own = 1.0, jax.random.fold_in(key, 6)
    for dim, parts in shards:
        heights = jnp.exp(jax.random.uniform(jax.random.fold_in(own, dim), (parts,), jnp.float32, least / len(shards), high / len(shards)))
        loudness = loudness * jnp.repeat(heights, shape[dim] // parts).reshape([-1 if axis == dim else 1 for axis in range(len(shape))])
    return loudness


def length_profile(count, total, bound, lean):
    portions = [(1 << 20) // math.isqrt(rank ** lean) + 1 for rank in range(2, count + 1)]
    spare, counts = total - bound - (count - 1), [1] * (count - 1)
    while spare > 0:
        movable = [i for i in range(count - 1) if counts[i] < bound]
        mass, budget = sum([portions[i] for i in movable]), spare
        for i in movable:
            more = min(bound - counts[i], max(1, budget * portions[i] // mass), spare)
            counts[i] = counts[i] + more
            spare = spare - more
    return np.array([bound] + counts)


def uneven(stream_key, amount, total, bound, slope):
    if amount == 2:
        one = jax.random.randint(stream_key, (), max(1, total - bound), min(bound, total - 1) + 1)
        return jnp.stack([one, total - one])
    tallies = jnp.asarray(length_profile(amount, total, bound, slope), jnp.int32)
    twos = (amount - 1) // 2
    giver, taker = tallies[1:1 + 2 * twos:2], tallies[2:2 + 2 * twos:2]
    margin = jnp.minimum(giver - 1, bound - taker)
    passed = jax.random.randint(jax.random.fold_in(stream_key, 1), (twos,), 0, 1 << 20) % (margin + 1)
    tallies = tallies.at[1:1 + 2 * twos:2].set(giver - passed).at[2:2 + 2 * twos:2].set(taker + passed)
    return tallies[jax.random.permutation(jax.random.fold_in(stream_key, 2), amount)]


def noise(own_key, dims, deviation, limit, cuts=(), kind=jnp.bfloat16):
    drawn = jax.random.normal(own_key, dims, jnp.float32) * deviation
    if len(cuts) > 0:
        drawn = block_levels(own_key, dims, cuts, -0.22, 0.18) * drawn
    return jnp.clip(drawn, min=-limit, max=limit).astype(kind)


def setup_inputs(seed: int = 0) -> dict:
    seeds = jax.random.split(jax.random.key(seed), 6)
    queries = draw_queries(jax.random.fold_in(seeds[5], 71), 0)
    keys = draw_keys(jax.random.fold_in(seeds[5], 71), 0)
    values = noise(seeds[2], (PACKED_TOKENS, KVH * HD), 1.0, 6.0, ((0, 8), (1, 4)))
    lengths = uneven(seeds[3], DOCS, PACKED_TOKENS, MOST, 2).astype(jnp.int32)
    out_weight = noise(seeds[4], (QH * HD, FEAT), 0.1, 0.59765625, ((0, 4),))
    return {"queries": queries, "keys": keys, "values": values, "lengths": lengths, "out_weight": out_weight}


def row_positions(rows):
    half_rows = TOK_DEV // 2
    device = rows // TOK_DEV
    offset = rows % TOK_DEV
    return jnp.where(offset < half_rows, device * half_rows + offset, (2 * N_CTX - 1 - device) * half_rows + offset - half_rows).astype(jnp.int32)


def position_rows(places):
    half_rows = TOK_DEV // 2
    block_num = places // half_rows
    offset = places % half_rows
    device = jnp.where(block_num < N_CTX, block_num, 2 * N_CTX - 1 - block_num)
    within = jnp.where(block_num < N_CTX, offset, offset + half_rows)
    return (device * TOK_DEV + within).astype(jnp.int32)


def doc_numbers(places, lengths):
    doc_ends = jnp.cumsum(lengths).astype(jnp.int32)
    return jnp.sum((places[:, None] >= doc_ends[None, :]).astype(jnp.int32), axis=1).astype(jnp.int32)


def reference(queries, keys, values, lengths, out_weight):
    group_size = QH // KVH
    score_scale = HD ** -0.5
    block_rows = TOK_DEV
    span_rows = MOST + block_rows
    places = jnp.arange(PACKED_TOKENS, dtype=jnp.int32)
    packed_rows = position_rows(places)
    q_packed = queries[packed_rows]
    k_packed = jnp.concatenate([jnp.zeros((MOST, KVH * HD), keys.dtype), keys[packed_rows]], axis=0)
    v_packed = jnp.concatenate([jnp.zeros((MOST, KVH * HD), values.dtype), values[packed_rows]], axis=0)
    doc_ids = doc_numbers(places, lengths)
    doc_padded = jnp.concatenate([jnp.full((MOST,), -1, jnp.int32), doc_ids])

    def attend_block(block_index):
        first_place = (block_index * block_rows).astype(jnp.int32)
        q_block = lax.dynamic_slice_in_dim(q_packed, first_place, block_rows, 0).reshape(block_rows, KVH, group_size, HD)
        k_block = lax.dynamic_slice_in_dim(k_packed, first_place, span_rows, 0).reshape(span_rows, KVH, HD)
        v_block = lax.dynamic_slice_in_dim(v_packed, first_place, span_rows, 0).reshape(span_rows, KVH, HD)
        q_doc = lax.dynamic_slice_in_dim(doc_ids, first_place, block_rows, 0)
        k_doc = lax.dynamic_slice_in_dim(doc_padded, first_place, span_rows, 0)
        q_place = first_place + jnp.arange(block_rows, dtype=jnp.int32)
        k_place = first_place - MOST + jnp.arange(span_rows, dtype=jnp.int32)
        allowed = (k_doc[None, :] == q_doc[:, None]) & (k_place[None, :] <= q_place[:, None])

        def one_head(number):
            q_head = lax.dynamic_index_in_dim(q_block, number, 1, keepdims=False)
            k_head = lax.dynamic_index_in_dim(k_block, number, 1, keepdims=False)
            v_head = lax.dynamic_index_in_dim(v_block, number, 1, keepdims=False)
            scores = jnp.einsum('tgd,pd->tgp', q_head.astype(jnp.float32), k_head.astype(jnp.float32)) * score_scale
            scores = jnp.where(allowed[:, None, :], scores, -1e30)
            row_max = jnp.max(scores, axis=2, keepdims=True)
            weights = jnp.where(allowed[:, None, :], jnp.exp(scores - row_max), 0.0)
            totals = jnp.sum(weights, axis=2)
            rounded = lax.optimization_barrier(weights.astype(jnp.bfloat16)).astype(jnp.float32)
            summed = jnp.einsum('tgp,pd->tgd', rounded, v_head.astype(jnp.float32))
            return summed / totals[..., None]

        per_head = lax.map(one_head, jnp.arange(KVH, dtype=jnp.int32))
        return jnp.transpose(per_head, (1, 0, 2, 3)).reshape(block_rows, QH * HD).astype(jnp.bfloat16)

    attended = lax.map(attend_block, jnp.arange(PACKED_TOKENS // block_rows, dtype=jnp.int32)).reshape(PACKED_TOKENS, QH * HD)
    attended = attended[row_positions(places)]
    group_rows = QH * HD // N_TP

    def add_group(group, total):
        first = (group * group_rows).astype(jnp.int32)
        part_cols = lax.dynamic_slice_in_dim(attended, first, group_rows, 1)
        part_rows = lax.dynamic_slice_in_dim(out_weight, first, group_rows, 0)
        partial_value = jnp.dot(part_cols, part_rows, preferred_element_type=jnp.float32)
        rounded = lax.optimization_barrier(partial_value.astype(jnp.bfloat16)).astype(jnp.float32)
        return total + rounded

    summed = lax.fori_loop(0, N_TP, add_group, jnp.zeros((PACKED_TOKENS, FEAT), jnp.float32))
    return summed.astype(jnp.bfloat16)
```

```python
import functools
import math

import jax
import jax.numpy as jnp
from jax import lax
from jax.experimental import pallas as pl
from jax.experimental.pallas import tpu as pltpu
from jax.sharding import PartitionSpec as P

QH = 64
KVH = 8
HD = 128
NEG = -1e30
MESH = pl.DeviceIdType.MESH
F32 = jnp.float32
BF16 = jnp.bfloat16


def kernel(
    n, t, chunk,
    len_ref, q_hbm, k_hbm, v_hbm, w_hbm,
    out_ref,
    q_s, kv_s, w_s, m_s, l_s, acc_s, att_s, own_s,
    mate_out, mate_in, far_out, far_in,
    q_sem, kv_sem, w_sem, send_sem, recv_sem,
    mate_send, mate_recv, far_send, far_recv,
):
    c = lax.axis_index("ctx")
    g = lax.axis_index("tp")
    o, i = c // 2, c % 2
    y, core = g // 2, g % 2
    m = n // 2
    ny = t // 2
    half = q_hbm.shape[0] // 2
    cuts = recv_sem.shape[2]
    cut = half // cuts
    kvw = k_hbm.shape[1]
    kvl = kvw // HD
    group = QH // KVH
    heads = kvl * group
    feat = w_hbm.shape[1] // t
    parts = feat // chunk
    factor = HD ** (-0.5) * math.log2(math.e)

    def q_copy(h, b):
        return pltpu.make_async_copy(
            q_hbm.at[pl.ds(b * half, half), pl.ds(h * HD, HD)],
            q_s.at[b, h // group, pl.ds((h % group) * half, half), :],
            q_sem.at[h, b],
        )

    def kv_copy(which, b):
        src = k_hbm if which == 0 else v_hbm
        return pltpu.make_async_copy(
            src.at[pl.ds(b * half, half), :],
            kv_s.at[o, b, pl.ds(i * half, half), pl.ds(which * kvw, kvw)],
            kv_sem.at[which, b],
        )

    for b in range(2):
        for which in range(2):
            kv_copy(which, b).start()
    barrier = pltpu.get_barrier_semaphore()

    def greet(**where):
        pl.semaphore_signal(barrier, inc=1, device_id=where, device_id_type=MESH)

    @pl.when(o + 1 < m)
    def _():
        greet(ctx=c + 2)

    @pl.when(o >= 1)
    def _():
        greet(ctx=c - 2)

    greet(ctx=o * 2 + 1 - i)
    greet(tp=y * 2 + 1 - core)
    for d in range(1, ny):
        greet(tp=((y + d) % ny) * 2 + core)
    for h in range(heads):
        for b in range(2):
            q_copy(h, b).start()
    w_copy = pltpu.make_async_copy(w_hbm, w_s, w_sem)
    w_copy.start()

    m_s[...] = jnp.full_like(m_s, NEG)
    l_s[...] = jnp.zeros_like(l_s)
    acc_s[...] = jnp.zeros_like(acc_s)

    longest = n * half * 2 * 3 // 4
    reach = (longest - 2) // half + 1

    def need_low(jo, target):
        return 2 * n - 1 - target - (2 * jo + 1) <= reach

    lacks_low = (i == 0) & jnp.logical_not(need_low(o, c))

    @pl.when(lacks_low)
    def _():
        kv_s[o, 0, half:, :] = jnp.zeros((half, 2 * kvw), BF16)

    @pl.when(i == 1)
    def _():
        kv_s[o, 1, :half, :] = jnp.zeros((half, 2 * kvw), BF16)

    def kv_piece(direction, jo, e, h):
        target = (c + 2, c - 2, o * 2 + 1 - i)[direction]
        rows = kv_s.at[jo, e, pl.ds(i * half + h * cut, cut), :]
        return pltpu.make_async_remote_copy(
            src_ref=rows,
            dst_ref=rows,
            send_sem=send_sem.at[direction, jo, e, h],
            recv_sem=recv_sem.at[jo * 2 + i, e, h],
            device_id={"ctx": target},
            device_id_type=MESH,
        )

    def kv_arrived(jo, k, e, h):
        rows = kv_s.at[jo, e, pl.ds(k * half + h * cut, cut), :]
        pltpu.make_async_remote_copy(
            src_ref=rows,
            dst_ref=rows,
            send_sem=send_sem.at[0, 0, 0, 0],
            recv_sem=recv_sem.at[jo * 2 + k, e, h],
            device_id={"ctx": o * 2 + 1 - i},
            device_id_type=MESH,
        ).wait_recv()

    def up(jo, act):
        @pl.when(o + 1 < m)
        def _():
            for h in range(cuts):
                act(kv_piece(0, jo, 0, h))

    def down(jo, e, act):
        @pl.when(o >= 1)
        def _():
            for h in range(cuts):
                act(kv_piece(1, jo, e, h))

    def across(jo, e, act):
        for h in range(cuts):
            act(kv_piece(2, jo, e, h))

    mate_lacks_low = (i == 1) & jnp.logical_not(need_low(o, c - 1))
    begin = lambda copy: copy.start()
    finish = lambda copy: copy.wait_send()

    def own_low(act):
        up(o, act)

        @pl.when(jnp.logical_not(mate_lacks_low))
        def _():
            across(o, 0, act)

        down(o, 0, act)

    def own_high(act):
        @pl.when(i == 1)
        def _():
            across(o, 1, act)

    ends = []
    total = jnp.int32(0)
    for d in range(len_ref.shape[0]):
        total = total + len_ref[d]
        ends.append(total)

    def attend(b, jo, e):
        q_first = jnp.where(b == 0, c, 2 * n - 1 - c) * half
        q_place = q_first + lax.broadcasted_iota(jnp.int32, (half, half), 0)
        start = jnp.zeros((half, half), jnp.int32)
        for end in ends:
            start = jnp.where(q_place >= end, end, start)
        biases = []
        for k in range(2):
            block = jnp.where(e == 0, 2 * jo + k, 2 * n - 1 - 2 * jo - k)
            k_place = block * half + lax.broadcasted_iota(jnp.int32, (half, half), 1)
            ok = (k_place >= start) & (k_place <= q_place)
            biases.append(jnp.where(ok, 0.0, NEG).astype(F32))
        for kh in range(kvl):
            q = q_s[b, kh]
            key = kv_s[jo, e, :, kh * HD:(kh + 1) * HD]
            s = lax.dot_general(q, key, (((1,), (1,)), ((), ())), preferred_element_type=F32)
            scores = []
            for k in range(2):
                part = s[:, k * half:(k + 1) * half].reshape(group, half, half) * factor + biases[k][None]
                scores.append(part.reshape(group * half, half))
            m_old = m_s[b, kh]
            m_new = jnp.maximum(m_old, jnp.max(jnp.maximum(*scores), axis=1, keepdims=True))
            alpha = jnp.exp2(m_old - m_new)
            ps = [jnp.exp2(part - m_new) for part in scores]
            m_s[b, kh] = m_new
            l_s[b, kh] = l_s[b, kh] * alpha + (ps[0] + ps[1])
            p = jnp.concatenate([part.astype(BF16) for part in ps], axis=1)
            value = kv_s[jo, e, :, kvw + kh * HD:kvw + (kh + 1) * HD]
            acc_s[b, kh] = acc_s[b, kh] * alpha + jnp.dot(p, value, preferred_element_type=F32)

    n_far = (ny - 1) * parts
    pieces = ny * parts

    def mate_copy(b, x):
        return pltpu.make_async_remote_copy(
            src_ref=mate_out.at[b, x],
            dst_ref=mate_in.at[b, x],
            send_sem=mate_send.at[b, x],
            recv_sem=mate_recv.at[b, x],
            device_id={"tp": y * 2 + 1 - core},
            device_id_type=MESH,
        )

    def far_copy(b, x):
        d = x // parts + 1
        return pltpu.make_async_remote_copy(
            src_ref=far_out.at[b, x],
            dst_ref=far_in.at[b, x],
            send_sem=far_send.at[b, x],
            recv_sem=far_recv.at[b, x],
            device_id={"tp": ((y + d) % ny) * 2 + core},
            device_id_type=MESH,
        )

    def normalize(b):
        for kh in range(kvl):
            inv = 1.0 / jnp.sum(l_s[b, kh], axis=1, keepdims=True)
            done = (acc_s[b, kh] * inv).astype(BF16)
            for r in range(group):
                h = kh * group + r
                att_s[:, h * HD:(h + 1) * HD] = done[r * half:(r + 1) * half]

    def piece(idx):
        b, x = idx // pieces, idx % pieces

        @pl.when(idx == 0)
        def _():
            w_copy.wait()

        @pl.when(x == 0)
        def _():
            normalize(b)

        d = jnp.where(x < n_far, x // parts + 1, 0)
        p = x % parts

        def term(k):
            first = (((y + d) % ny) * 2 + k) * feat + p * chunk
            cols = pl.ds(pl.multiple_of(first, chunk), chunk)
            return jnp.dot(att_s[...], w_s[:, cols], preferred_element_type=F32)

        mate_out[b, x] = term(1 - core).astype(BF16)
        mate_copy(b, x).start()

        @pl.when((x >= 1) & (x <= n_far))
        def _():
            mate_copy(b, x - 1).wait_recv()
            far_out[b, x - 1] = (own_s[b, x - 1] + mate_in[b, x - 1].astype(F32)).astype(BF16)
            far_copy(b, x - 1).start()

        own_s[b, x] = term(core)

    def mate_low(jo):
        for h in range(cuts):
            kv_arrived(jo, 1 - i, 0, h)

    def attend_low(d):
        jo = o - d

        @pl.when((d > 0) | jnp.logical_not(lacks_low))
        def _():
            mate_low(jo)

        def one(b, carry):
            attend(b, jo, 0)
            return carry

        lax.fori_loop(0, jnp.where(need_low(jo, c), 2, 1), one, 0)

    def receive_low(d):
        jo = o - d
        for h in range(cuts):
            kv_arrived(jo, i, 0, h)

            @pl.when(o + 1 < m)
            def _():
                kv_piece(0, jo, 0, h).start()

            kv_piece(2, jo, 0, h).start()

    above = 2 * (m - 1 - o)

    def receive_above(k):
        jo, e = o + 1 + k // 2, k % 2
        for h in range(cuts):
            kv_arrived(jo, i, e, h)

            @pl.when(o >= 1)
            def _():
                kv_piece(1, jo, e, h).start()

            kv_piece(2, jo, e, h).start()

    def attend_high(jo, e):
        @pl.when((jo > o) | (i == 0))
        def _():
            for h in range(cuts):
                kv_arrived(jo, 1 - i, e, h)

        attend(1, jo, e)

    for b in range(2):
        for which in range(2):
            kv_copy(which, b).wait()
    line = jnp.where(o + 1 < m, 1, 0) + jnp.where(o >= 1, 1, 0)
    pl.semaphore_wait(barrier, line + 1 + ny)
    own_low(begin)
    down(o, 1, begin)
    for h in range(heads):
        for b in range(2):
            q_copy(h, b).wait()

    def low_step(d, carry):
        @pl.when(d < o)
        def _():
            receive_low(d + 1)

        @pl.when(d == o)
        def _():
            own_high(begin)

            def early(k, inner):
                receive_above(k)
                return inner

            lax.fori_loop(0, jnp.minimum(above, 2), early, 0)

        attend_low(d)
        return carry

    lax.fori_loop(0, o + 1, low_step, 0)

    def next_piece(idx, carry):
        piece(idx)
        return carry

    beside = jnp.clip(above - 2, 0, pieces)
    lax.fori_loop(0, pieces - beside, next_piece, 0)

    def high_step(k, carry):
        idx = k - 2

        @pl.when(idx < beside)
        def _():
            piece(pieces - beside + idx)

        @pl.when(k < above)
        def _():
            receive_above(k)

        def high(x, inner):
            inside = x == 0
            attend_high(jnp.where(inside, o, o + 1 + idx // 2), jnp.where(inside, 1, idx % 2))
            return inner

        lax.fori_loop(jnp.where(idx == 0, 0, 1), jnp.where(idx < above, 2, 1), high, 0)
        return carry

    lax.fori_loop(2, jnp.maximum(above, 1) + 2, high_step, 0)
    lax.fori_loop(pieces, 2 * pieces, next_piece, 0)

    for b in range(2):
        for p in range(parts):
            x = n_far + p
            mate_copy(b, x).wait_recv()
            whole = own_s[b, x] + mate_in[b, x].astype(F32)
            for d in range(1, ny):
                z = (d - 1) * parts + p
                far_copy(b, z).wait_recv()
                whole = whole + far_in[b, z].astype(F32)
            out_ref[b * half:(b + 1) * half, p * chunk:(p + 1) * chunk] = whole.astype(BF16)

    for b in range(2):
        for x in range(pieces):
            mate_copy(b, x).wait_send()
        for x in range(n_far):
            far_copy(b, x).wait_send()

    own_low(finish)
    own_high(finish)
    down(o, 1, finish)

    def drain_low(jo, carry):
        up(jo, finish)
        across(jo, 0, finish)
        return carry

    lax.fori_loop(0, o, drain_low, 0)

    def drain_above(jo, carry):
        for e in range(2):
            down(jo, e, finish)
            across(jo, e, finish)
        return carry

    lax.fori_loop(o + 1, m, drain_above, 0)


def solution(mesh):
    n, t = mesh.shape["ctx"], mesh.shape["tp"]

    def on_device(queries, keys, values, lengths, out_weight):
        rows, width = queries.shape
        half = rows // 2
        kvw = keys.shape[1]
        kvl = kvw // HD
        group = QH // KVH
        heads = width // HD
        feat = out_weight.shape[1] // t
        chunk = min(feat, 512)
        pieces = (t // 2) * (feat // chunk)
        far = max(1, (t // 2 - 1) * (feat // chunk))
        cuts = 2
        dma = pltpu.SemaphoreType.DMA
        hbm = pl.BlockSpec(memory_space=pl.ANY)
        return pl.pallas_call(
            functools.partial(kernel, n, t, chunk),
            out_shape=jax.ShapeDtypeStruct((rows, feat), BF16),
            in_specs=[pl.BlockSpec(memory_space=pltpu.SMEM), hbm, hbm, hbm, hbm],
            out_specs=pl.BlockSpec(memory_space=pltpu.VMEM),
            scratch_shapes=[
                pltpu.VMEM((2, kvl, group * half, HD), BF16),
                pltpu.VMEM((n // 2, 2, 2 * half, 2 * kvw), BF16),
                pltpu.VMEM(out_weight.shape, BF16),
                pltpu.VMEM((2, kvl, group * half, half), F32),
                pltpu.VMEM((2, kvl, group * half, half), F32),
                pltpu.VMEM((2, kvl, group * half, HD), F32),
                pltpu.VMEM((half, width), BF16),
                pltpu.VMEM((2, pieces, half, chunk), F32),
                pltpu.VMEM((2, pieces, half, chunk), BF16),
                pltpu.VMEM((2, pieces, half, chunk), BF16),
                pltpu.VMEM((2, far, half, chunk), BF16),
                pltpu.VMEM((2, far, half, chunk), BF16),
                dma((heads, 2)),
                dma((2, 2)),
                dma,
                dma((3, n // 2, 2, cuts)),
                dma((n, 2, cuts)),
                dma((2, pieces)),
                dma((2, pieces)),
                dma((2, far)),
                dma((2, far)),
            ],
            compiler_params=pltpu.CompilerParams(
                collective_id=0, has_side_effects=True, vmem_limit_bytes=60 * 1024 * 1024
            ),
        )(lengths, queries, keys, values, out_weight)

    return jax.shard_map(
        on_device,
        mesh=mesh,
        in_specs=(P("ctx", "tp"), P("ctx", "tp"), P("ctx", "tp"), P(), P("tp", None)),
        out_specs=P("ctx", "tp"),
        check_vma=False,
    )
```

```python
import functools
import math

import jax
import jax.numpy as jnp
from jax import lax
from jax.experimental import pallas as pl
from jax.experimental.pallas import tpu as pltpu
from jax.sharding import PartitionSpec as P

QH = 64
KVH = 8
HD = 128
NEG = -1e30
MESH = pl.DeviceIdType.MESH
F32 = jnp.float32
BF16 = jnp.bfloat16


def kernel(
    n, t, chunk,
    len_ref, q_hbm, k_hbm, v_hbm, w_hbm,
    near_ref, far_ref,
    q_s, kv_s, w_s, m_s, l_s, acc_s, att_s, own_s,
    mate_out, mate_in, far_out,
    q_sem, kv_sem, w_sem, send_sem, recv_sem,
    mate_send, mate_recv, far_send, far_recv,
):
    c = lax.axis_index("ctx")
    g = lax.axis_index("tp")
    o, i = c // 2, c % 2
    y, core = g // 2, g % 2
    m = n // 2
    ny = t // 2
    half = q_hbm.shape[0] // 2
    cuts = recv_sem.shape[2]
    cut = half // cuts
    kvw = k_hbm.shape[1]
    kvl = kvw // HD
    group = QH // KVH
    heads = kvl * group
    feat = w_hbm.shape[1] // t
    parts = feat // chunk
    factor = HD ** (-0.5) * math.log2(math.e)

    def q_copy(h, b):
        return pltpu.make_async_copy(
            q_hbm.at[pl.ds(b * half, half), pl.ds(h * HD, HD)],
            q_s.at[b, h // group, pl.ds((h % group) * half, half), :],
            q_sem.at[h, b],
        )

    def kv_copy(which, b):
        src = k_hbm if which == 0 else v_hbm
        return pltpu.make_async_copy(
            src.at[pl.ds(b * half, half), :],
            kv_s.at[o, b, pl.ds(i * half, half), pl.ds(which * kvw, kvw)],
            kv_sem.at[which, b],
        )

    for b in range(2):
        for which in range(2):
            kv_copy(which, b).start()
    barrier = pltpu.get_barrier_semaphore()

    def greet(**where):
        pl.semaphore_signal(barrier, inc=1, device_id=where, device_id_type=MESH)

    @pl.when(o + 1 < m)
    def _():
        greet(ctx=c + 2)

    @pl.when(o >= 1)
    def _():
        greet(ctx=c - 2)

    greet(ctx=o * 2 + 1 - i)
    greet(tp=y * 2 + 1 - core)
    for d in range(1, ny):
        greet(tp=((y + d) % ny) * 2 + core)
    for h in range(heads):
        for b in range(2):
            q_copy(h, b).start()
    w_copy = pltpu.make_async_copy(w_hbm, w_s, w_sem)
    w_copy.start()

    m_s[...] = jnp.full_like(m_s, NEG)
    l_s[...] = jnp.zeros_like(l_s)
    acc_s[...] = jnp.zeros_like(acc_s)

    longest = n * half * 2 * 3 // 4
    reach = (longest - 2) // half + 1

    def need_low(jo, target):
        return 2 * n - 1 - target - (2 * jo + 1) <= reach

    lacks_low = (i == 0) & jnp.logical_not(need_low(o, c))

    @pl.when(lacks_low)
    def _():
        kv_s[o, 0, half:, :] = jnp.zeros((half, 2 * kvw), BF16)

    @pl.when(i == 1)
    def _():
        kv_s[o, 1, :half, :] = jnp.zeros((half, 2 * kvw), BF16)

    def kv_piece(direction, jo, e, h):
        target = (c + 2, c - 2, o * 2 + 1 - i)[direction]
        rows = kv_s.at[jo, e, pl.ds(i * half + h * cut, cut), :]
        return pltpu.make_async_remote_copy(
            src_ref=rows,
            dst_ref=rows,
            send_sem=send_sem.at[direction, jo, e, h],
            recv_sem=recv_sem.at[jo * 2 + i, e, h],
            device_id={"ctx": target},
            device_id_type=MESH,
        )

    def kv_arrived(jo, k, e, h):
        rows = kv_s.at[jo, e, pl.ds(k * half + h * cut, cut), :]
        pltpu.make_async_remote_copy(
            src_ref=rows,
            dst_ref=rows,
            send_sem=send_sem.at[0, 0, 0, 0],
            recv_sem=recv_sem.at[jo * 2 + k, e, h],
            device_id={"ctx": o * 2 + 1 - i},
            device_id_type=MESH,
        ).wait_recv()

    def up(jo, act):
        @pl.when(o + 1 < m)
        def _():
            for h in range(cuts):
                act(kv_piece(0, jo, 0, h))

    def down(jo, e, act):
        @pl.when(o >= 1)
        def _():
            for h in range(cuts):
                act(kv_piece(1, jo, e, h))

    def across(jo, e, act):
        for h in range(cuts):
            act(kv_piece(2, jo, e, h))

    mate_lacks_low = (i == 1) & jnp.logical_not(need_low(o, c - 1))
    begin = lambda copy: copy.start()
    finish = lambda copy: copy.wait_send()

    def own_low(act):
        up(o, act)

        @pl.when(jnp.logical_not(mate_lacks_low))
        def _():
            across(o, 0, act)

        down(o, 0, act)

    def own_high(act):
        @pl.when(i == 1)
        def _():
            across(o, 1, act)

    ends = []
    total = jnp.int32(0)
    for d in range(len_ref.shape[0]):
        total = total + len_ref[d]
        ends.append(total)

    def attend(b, jo, e):
        q_first = jnp.where(b == 0, c, 2 * n - 1 - c) * half
        q_place = q_first + lax.broadcasted_iota(jnp.int32, (half, half), 0)
        start = jnp.zeros((half, half), jnp.int32)
        for end in ends:
            start = jnp.where(q_place >= end, end, start)
        biases = []
        for k in range(2):
            block = jnp.where(e == 0, 2 * jo + k, 2 * n - 1 - 2 * jo - k)
            k_place = block * half + lax.broadcasted_iota(jnp.int32, (half, half), 1)
            ok = (k_place >= start) & (k_place <= q_place)
            biases.append(jnp.where(ok, 0.0, NEG).astype(F32))
        for kh in range(kvl):
            q = q_s[b, kh]
            key = kv_s[jo, e, :, kh * HD:(kh + 1) * HD]
            s = lax.dot_general(q, key, (((1,), (1,)), ((), ())), preferred_element_type=F32)
            scores = []
            for k in range(2):
                part = s[:, k * half:(k + 1) * half].reshape(group, half, half) * factor + biases[k][None]
                scores.append(part.reshape(group * half, half))
            m_old = m_s[b, kh]
            m_new = jnp.maximum(m_old, jnp.max(jnp.maximum(*scores), axis=1, keepdims=True))
            alpha = jnp.exp2(m_old - m_new)
            ps = [jnp.exp2(part - m_new) for part in scores]
            m_s[b, kh] = m_new
            l_s[b, kh] = l_s[b, kh] * alpha + (ps[0] + ps[1])
            p = jnp.concatenate([part.astype(BF16) for part in ps], axis=1)
            value = kv_s[jo, e, :, kvw + kh * HD:kvw + (kh + 1) * HD]
            acc_s[b, kh] = acc_s[b, kh] * alpha + jnp.dot(p, value, preferred_element_type=F32)

    n_far = (ny - 1) * parts
    pieces = ny * parts

    def mate_copy(b, x):
        return pltpu.make_async_remote_copy(
            src_ref=mate_out.at[b, x],
            dst_ref=mate_in.at[b, x],
            send_sem=mate_send.at[b, x],
            recv_sem=mate_recv.at[b, x],
            device_id={"tp": y * 2 + 1 - core},
            device_id_type=MESH,
        )

    def far_copy(b, x):
        d = x // parts + 1
        return pltpu.make_async_remote_copy(
            src_ref=far_out.at[b, x],
            dst_ref=far_ref.at[d - 1, pl.ds(b * half, half), pl.ds(pl.multiple_of((x % parts) * chunk, chunk), chunk)],
            send_sem=far_send.at[b, x],
            recv_sem=far_recv.at[b, x],
            device_id={"tp": ((y + d) % ny) * 2 + core},
            device_id_type=MESH,
        )

    def normalize(b):
        for kh in range(kvl):
            inv = 1.0 / jnp.sum(l_s[b, kh], axis=1, keepdims=True)
            done = (acc_s[b, kh] * inv).astype(BF16)
            for r in range(group):
                h = kh * group + r
                att_s[:, h * HD:(h + 1) * HD] = done[r * half:(r + 1) * half]

    def piece(idx):
        b, x = idx // pieces, idx % pieces

        @pl.when(idx == 0)
        def _():
            w_copy.wait()

        @pl.when(x == 0)
        def _():
            normalize(b)

        d = jnp.where(x < n_far, x // parts + 1, 0)
        p = x % parts

        def term(k):
            first = (((y + d) % ny) * 2 + k) * feat + p * chunk
            cols = pl.ds(pl.multiple_of(first, chunk), chunk)
            return jnp.dot(att_s[...], w_s[:, cols], preferred_element_type=F32)

        mate_out[b, x] = term(1 - core).astype(BF16)
        mate_copy(b, x).start()

        @pl.when((x >= 1) & (x <= n_far))
        def _():
            mate_copy(b, x - 1).wait_recv()
            far_out[b, x - 1] = (own_s[b, x - 1] + mate_in[b, x - 1].astype(F32)).astype(BF16)
            far_copy(b, x - 1).start()

        own_s[b, x] = term(core)

    def mate_low(jo):
        for h in range(cuts):
            kv_arrived(jo, 1 - i, 0, h)

    def attend_low(d):
        jo = o - d

        @pl.when((d > 0) | jnp.logical_not(lacks_low))
        def _():
            mate_low(jo)

        def one(b, carry):
            attend(b, jo, 0)
            return carry

        lax.fori_loop(0, jnp.where(need_low(jo, c), 2, 1), one, 0)

    def receive_low(d):
        jo = o - d
        for h in range(cuts):
            kv_arrived(jo, i, 0, h)

            @pl.when(o + 1 < m)
            def _():
                kv_piece(0, jo, 0, h).start()

            kv_piece(2, jo, 0, h).start()

    above = 2 * (m - 1 - o)

    def receive_above(k, h):
        jo, e = o + 1 + k // 2, k % 2
        kv_arrived(jo, i, e, h)

        @pl.when(o >= 1)
        def _():
            kv_piece(1, jo, e, h).start()

        kv_piece(2, jo, e, h).start()

    def attend_high(jo, e):
        @pl.when((jo > o) | (i == 0))
        def _():
            for h in range(cuts):
                kv_arrived(jo, 1 - i, e, h)

        attend(1, jo, e)

    for b in range(2):
        for which in range(2):
            kv_copy(which, b).wait()
    line = jnp.where(o + 1 < m, 1, 0) + jnp.where(o >= 1, 1, 0)
    pl.semaphore_wait(barrier, line + 1 + ny)
    own_low(begin)
    down(o, 1, begin)
    for h in range(heads):
        for b in range(2):
            q_copy(h, b).wait()

    def low_step(d, carry):
        @pl.when(d < o)
        def _():
            receive_low(d + 1)

        @pl.when(d == jnp.maximum(o - 1, 0))
        def _():
            own_high(begin)

            def early(k, inner):
                for h in range(cuts):
                    receive_above(k, h)
                return inner

            lax.fori_loop(0, jnp.minimum(above, 2), early, 0)

        attend_low(d)
        return carry

    lax.fori_loop(0, o + 1, low_step, 0)

    def next_piece(idx, carry):
        piece(idx)
        return carry

    dense = above >= pieces + 2
    per = (pieces + 1) // 2
    lax.fori_loop(0, jnp.where(above > 2, 0, pieces), next_piece, 0)

    def some_pieces(first, last):
        lax.fori_loop(jnp.clip(first, 0, pieces), jnp.clip(last, 0, pieces), next_piece, 0)

    def high_step(k, carry):
        idx = k - 2
        for h in range(cuts):
            @pl.when(k < above)
            def _():
                receive_above(k, h)

            if h == 0:
                first = jnp.where(dense, idx, jnp.where(above > 2, (k - above) * per, pieces))
                some_pieces(first, first + jnp.where(dense, 1, per))

        def high(x, inner):
            inside = x == 0
            attend_high(jnp.where(inside, o, o + 1 + idx // 2), jnp.where(inside, 1, idx % 2))
            return inner

        lax.fori_loop(jnp.where(idx == 0, 0, 1), jnp.where(idx < above, 2, 1), high, 0)
        return carry

    lax.fori_loop(2, jnp.maximum(above, 1) + 2, high_step, 0)
    lax.fori_loop(pieces, 2 * pieces, next_piece, 0)

    for b in range(2):
        for p in range(parts):
            x = n_far + p
            mate_copy(b, x).wait_recv()
            near_ref[b * half:(b + 1) * half, p * chunk:(p + 1) * chunk] = own_s[b, x] + mate_in[b, x].astype(F32)
    for b in range(2):
        for x in range(n_far):
            far_copy(b, x).wait_recv()

    for b in range(2):
        for x in range(pieces):
            mate_copy(b, x).wait_send()
        for x in range(n_far):
            far_copy(b, x).wait_send()

    own_low(finish)
    own_high(finish)
    down(o, 1, finish)

    def drain_low(jo, carry):
        up(jo, finish)
        across(jo, 0, finish)
        return carry

    lax.fori_loop(0, o, drain_low, 0)

    def drain_above(jo, carry):
        for e in range(2):
            down(jo, e, finish)
            across(jo, e, finish)
        return carry

    lax.fori_loop(o + 1, m, drain_above, 0)


def solution(mesh):
    n, t = mesh.shape["ctx"], mesh.shape["tp"]

    def on_device(queries, keys, values, lengths, out_weight):
        rows, width = queries.shape
        half = rows // 2
        kvw = keys.shape[1]
        kvl = kvw // HD
        group = QH // KVH
        heads = width // HD
        feat = out_weight.shape[1] // t
        chunk = min(feat, 512)
        pieces = (t // 2) * (feat // chunk)
        far = max(1, (t // 2 - 1) * (feat // chunk))
        cuts = 2
        dma = pltpu.SemaphoreType.DMA
        hbm = pl.BlockSpec(memory_space=pl.ANY)
        near, others = pl.pallas_call(
            functools.partial(kernel, n, t, chunk),
            out_shape=[
                pltpu.VMEM((rows, feat), F32),
                pltpu.VMEM((max(1, t // 2 - 1), rows, feat), BF16),
            ],
            in_specs=[pl.BlockSpec(memory_space=pltpu.SMEM), hbm, hbm, hbm, hbm],
            out_specs=[pl.BlockSpec(memory_space=pltpu.VMEM)] * 2,
            scratch_shapes=[
                pltpu.VMEM((2, kvl, group * half, HD), BF16),
                pltpu.VMEM((n // 2, 2, 2 * half, 2 * kvw), BF16),
                pltpu.VMEM(out_weight.shape, BF16),
                pltpu.VMEM((2, kvl, group * half, half), F32),
                pltpu.VMEM((2, kvl, group * half, half), F32),
                pltpu.VMEM((2, kvl, group * half, HD), F32),
                pltpu.VMEM((half, width), BF16),
                pltpu.VMEM((2, pieces, half, chunk), F32),
                pltpu.VMEM((2, pieces, half, chunk), BF16),
                pltpu.VMEM((2, pieces, half, chunk), BF16),
                pltpu.VMEM((2, far, half, chunk), BF16),
                dma((heads, 2)),
                dma((2, 2)),
                dma,
                dma((3, n // 2, 2, cuts)),
                dma((n, 2, cuts)),
                dma((2, pieces)),
                dma((2, pieces)),
                dma((2, far)),
                dma((2, far)),
            ],
            compiler_params=pltpu.CompilerParams(
                collective_id=0, has_side_effects=True, vmem_limit_bytes=56 * 1024 * 1024
            ),
        )(lengths, queries, keys, values, out_weight)
        return (near + jnp.sum(others.astype(F32), axis=0)).astype(BF16)

    return jax.shard_map(
        on_device,
        mesh=mesh,
        in_specs=(P("ctx", "tp"), P("ctx", "tp"), P("ctx", "tp"), P(), P("tp", None)),
        out_specs=P("ctx", "tp"),
        check_vma=False,
    )
```

```python
import functools
import math

import jax
import jax.numpy as jnp
from jax import lax
from jax.experimental import pallas as pl
from jax.experimental.pallas import tpu as pltpu
from jax.sharding import PartitionSpec as P

QH = 64
KVH = 8
HD = 128
NEG = -1e30
MESH = pl.DeviceIdType.MESH
F32 = jnp.float32
BF16 = jnp.bfloat16


def kernel(
    n, t, chunk,
    len_ref, q_hbm, k_hbm, v_hbm, w_hbm,
    near_ref, far_ref,
    q_s, kv_s, w_s, m_s, l_s, acc_s, att_s, own_s, first_s,
    mate_out, mate_in, far_out,
    q_sem, kv_sem, w_sem, send_sem, recv_sem,
    mate_send, mate_recv, far_send, far_recv,
):
    c = lax.axis_index("ctx")
    g = lax.axis_index("tp")
    o, i = c // 2, c % 2
    y, core = g // 2, g % 2
    m = n // 2
    ny = t // 2
    half = q_hbm.shape[0] // 2
    cuts = recv_sem.shape[2]
    kvw = k_hbm.shape[1]
    kvl = kvw // HD
    group = QH // KVH
    heads = kvl * group
    feat = w_hbm.shape[1] // t
    parts = feat // chunk
    factor = HD ** (-0.5) * math.log2(math.e)

    def q_copy(h, b):
        return pltpu.make_async_copy(
            q_hbm.at[pl.ds(b * half, half), pl.ds(h * HD, HD)],
            q_s.at[b, h // group, pl.ds((h % group) * half, half), :],
            q_sem.at[h, b],
        )

    def kv_copy(which, b, h):
        src = k_hbm if which == 0 else v_hbm
        return pltpu.make_async_copy(
            src.at[pl.ds(b * half, half), pl.ds(h * HD, HD)],
            kv_s.at[o, b, pl.ds(i * half, half), pl.ds((2 * h + which) * HD, HD)],
            kv_sem.at[which, b, h],
        )

    own = [(which, b, h) for b in range(2) for h in range(kvl) for which in range(2)]
    for part in own:
        kv_copy(*part).start()
    barrier = pltpu.get_barrier_semaphore()

    def greet(**where):
        pl.semaphore_signal(barrier, inc=1, device_id=where, device_id_type=MESH)

    @pl.when(o + 1 < m)
    def _():
        greet(ctx=c + 2)

    @pl.when(o >= 1)
    def _():
        greet(ctx=c - 2)

    greet(ctx=o * 2 + 1 - i)
    greet(tp=y * 2 + 1 - core)
    for d in range(1, ny):
        greet(tp=((y + d) % ny) * 2 + core)
    w_copy = pltpu.make_async_copy(w_hbm, w_s, w_sem)
    longest = n * half * 2 * 3 // 4
    reach = (longest - 2) // half + 1

    def need_low(jo, target):
        return 2 * n - 1 - target - (2 * jo + 1) <= reach

    lacks_low = (i == 0) & jnp.logical_not(need_low(o, c))

    def kv_piece(direction, jo, e, h):
        target = (c + 2, c - 2, o * 2 + 1 - i)[direction]
        rows = kv_s.at[jo, e, pl.ds(i * half, half), pl.ds(h * 2 * HD, 2 * HD)]
        return pltpu.make_async_remote_copy(
            src_ref=rows,
            dst_ref=rows,
            send_sem=send_sem.at[direction, jo, e, h],
            recv_sem=recv_sem.at[jo * 2 + i, e, h],
            device_id={"ctx": target},
            device_id_type=MESH,
        )

    def kv_arrived(jo, k, e, h):
        rows = kv_s.at[jo, e, pl.ds(k * half, half), pl.ds(h * 2 * HD, 2 * HD)]
        pltpu.make_async_remote_copy(
            src_ref=rows,
            dst_ref=rows,
            send_sem=send_sem.at[0, 0, 0, 0],
            recv_sem=recv_sem.at[jo * 2 + k, e, h],
            device_id={"ctx": o * 2 + 1 - i},
            device_id_type=MESH,
        ).wait_recv()

    def up(jo, act):
        @pl.when(o + 1 < m)
        def _():
            for h in range(cuts):
                act(kv_piece(0, jo, 0, h))

    def down(jo, e, act):
        @pl.when(o >= 1)
        def _():
            for h in range(cuts):
                act(kv_piece(1, jo, e, h))

    def across(jo, e, act):
        for h in range(cuts):
            act(kv_piece(2, jo, e, h))

    mate_lacks_low = (i == 1) & jnp.logical_not(need_low(o, c - 1))
    begin = lambda copy: copy.start()
    finish = lambda copy: copy.wait_send()

    def own_low(act):
        up(o, act)

        @pl.when(jnp.logical_not(mate_lacks_low))
        def _():
            across(o, 0, act)

        down(o, 0, act)

    def own_high(act):
        @pl.when(i == 1)
        def _():
            across(o, 1, act)

    ends = []
    total = jnp.int32(0)
    for d in range(len_ref.shape[0]):
        total = total + len_ref[d]
        ends.append(total)

    def attend(b, jo, e, ready=None, after=None):
        q_first = jnp.where(b == 0, c, 2 * n - 1 - c) * half
        q_place = q_first + lax.broadcasted_iota(jnp.int32, (half, half), 0)
        start = jnp.zeros((half, half), jnp.int32)
        for end in ends:
            start = jnp.where(q_place >= end, end, start)
        biases = []
        for k in range(2):
            block = jnp.where(e == 0, 2 * jo + k, 2 * n - 1 - 2 * jo - k)
            k_place = block * half + lax.broadcasted_iota(jnp.int32, (half, half), 1)
            ok = (k_place >= start) & (k_place <= q_place)
            biases.append(jnp.where(ok, 0.0, NEG).astype(F32))
        for kh in range(kvl):
            if ready is not None:
                ready(kh)
            q = q_s[b, kh]
            key = kv_s[jo, e, :, 2 * kh * HD:(2 * kh + 1) * HD]
            s = lax.dot_general(q, key, (((1,), (1,)), ((), ())), preferred_element_type=F32)
            scores = []
            for k in range(2):
                part = s[:, k * half:(k + 1) * half].reshape(group, half, half) * factor + biases[k][None]
                scores.append(part.reshape(group * half, half))
            m_old = m_s[b, kh]
            m_new = jnp.maximum(m_old, jnp.max(jnp.maximum(*scores), axis=1, keepdims=True))
            alpha = jnp.exp2(m_old - m_new)
            ps = [jnp.exp2(part - m_new) for part in scores]
            m_s[b, kh] = m_new
            l_s[b, kh] = l_s[b, kh] * alpha + (ps[0] + ps[1])
            p = jnp.concatenate([part.astype(BF16) for part in ps], axis=1)
            value = kv_s[jo, e, :, (2 * kh + 1) * HD:(2 * kh + 2) * HD]
            acc_s[b, kh] = acc_s[b, kh] * alpha + jnp.dot(p, value, preferred_element_type=F32)
            if after is not None:
                after(kh)

    n_far = (ny - 1) * parts
    pieces = ny * parts

    def mate_copy(b, x):
        return pltpu.make_async_remote_copy(
            src_ref=mate_out.at[b, x],
            dst_ref=mate_in.at[b, x],
            send_sem=mate_send.at[b, x],
            recv_sem=mate_recv.at[b, x],
            device_id={"tp": y * 2 + 1 - core},
            device_id_type=MESH,
        )

    def far_copy(b, x):
        d = x // parts + 1
        return pltpu.make_async_remote_copy(
            src_ref=far_out.at[b, x],
            dst_ref=far_ref.at[d - 1, pl.ds(b * half, half), pl.ds(pl.multiple_of((x % parts) * chunk, chunk), chunk)],
            send_sem=far_send.at[b, x],
            recv_sem=far_recv.at[b, x],
            device_id={"tp": ((y + d) % ny) * 2 + core},
            device_id_type=MESH,
        )

    def normalize(b, kh):
        inv = 1.0 / jnp.sum(l_s[b, kh], axis=1, keepdims=True)
        done = (acc_s[b, kh] * inv).astype(BF16)
        for r in range(group):
            h = kh * group + r
            att_s[:, h * HD:(h + 1) * HD] = done[r * half:(r + 1) * half]

    span = group * HD

    def first_products(kh):
        normalize(1, kh)
        for number, (x, mine) in enumerate(((0, False), (0, True), (1, False))):
            d = x // parts + 1 if x < n_far else 0
            first = (((y + d) % ny) * 2 + (core if mine else 1 - core)) * feat + (x % parts) * chunk
            cols = pl.ds(pl.multiple_of(first, chunk), chunk)
            rows = slice(kh * span, (kh + 1) * span)
            value = jnp.dot(att_s[:, rows], w_s[rows, cols], preferred_element_type=F32)
            if kh > 0:
                value = value + first_s[number]
            if kh < kvl - 1:
                first_s[number] = value
            elif mine:
                own_s[1, x] = value
            else:
                mate_out[1, x] = value.astype(BF16)
                mate_copy(1, x).start()

    def piece(idx):
        b, x = idx // pieces, idx % pieces

        @pl.when(idx == 0)
        def _():
            w_copy.wait()

        @pl.when(x == 0)
        def _():
            for kh in range(kvl):
                normalize(b, kh)
            first = (((y + jnp.where(n_far > 0, 1, 0)) % ny) * 2 + 1 - core) * feat
            cols = pl.ds(pl.multiple_of(first, chunk), chunk)
            mate_out[b, 0] = jnp.dot(att_s[...], w_s[:, cols], preferred_element_type=F32).astype(BF16)

        d = jnp.where(x < n_far, x // parts + 1, 0)
        p = x % parts

        def term(k):
            first = (((y + d) % ny) * 2 + k) * feat + p * chunk
            cols = pl.ds(pl.multiple_of(first, chunk), chunk)
            return jnp.dot(att_s[...], w_s[:, cols], preferred_element_type=F32)

        @pl.when((x > 0) & (idx != pieces + 1))
        def _():
            mate_out[b, x] = term(1 - core).astype(BF16)

        @pl.when(idx != pieces + 1)
        def _():
            mate_copy(b, x).start()

        @pl.when((x >= 1) & (x <= n_far))
        def _():
            mate_copy(b, x - 1).wait_recv()
            far_out[b, x - 1] = (own_s[b, x - 1] + mate_in[b, x - 1].astype(F32)).astype(BF16)
            far_copy(b, x - 1).start()

        own_s[b, x] = term(core)

    def mate_low(jo):
        for h in range(cuts):
            kv_arrived(jo, 1 - i, 0, h)

    def attend_low(d):
        jo = o - d

        @pl.when((d > 0) | jnp.logical_not(lacks_low))
        def _():
            mate_low(jo)

        def one(b, carry):
            attend(b, jo, 0)
            return carry

        lax.fori_loop(0, jnp.where(need_low(jo, c), 2, 1), one, 0)

    def receive_low(d):
        jo = o - d
        for h in range(cuts):
            kv_arrived(jo, i, 0, h)

            @pl.when(o + 1 < m)
            def _():
                kv_piece(0, jo, 0, h).start()

            kv_piece(2, jo, 0, h).start()

    above = 2 * (m - 1 - o)

    def receive_above(k, h):
        jo, e = o + 1 + k // 2, k % 2
        kv_arrived(jo, i, e, h)

        @pl.when(o >= 1)
        def _():
            kv_piece(1, jo, e, h).start()

        kv_piece(2, jo, e, h).start()

    def attend_high(jo, e):
        @pl.when((jo > o) | (i == 0))
        def _():
            for h in range(cuts):
                kv_arrived(jo, 1 - i, e, h)

        attend(1, jo, e)

    def attend_last():
        jo = jnp.where(above > 0, m - 1, o)

        def ready(kh):
            @pl.when((above > 0) | (i == 0))
            def _():
                kv_arrived(jo, 1 - i, 1, kh)

        attend(1, jo, 1, ready, first_products)

    for part in own:
        kv_copy(*part).wait()
    line = jnp.where(o + 1 < m, 1, 0) + jnp.where(o >= 1, 1, 0)
    pl.semaphore_wait(barrier, line + 1 + ny)
    own_low(begin)
    down(o, 1, begin)
    for h in range(heads):
        for b in range(2):
            q_copy(h, b).start()
    w_copy.start()
    m_s[...] = jnp.full_like(m_s, NEG)
    l_s[...] = jnp.zeros_like(l_s)
    acc_s[...] = jnp.zeros_like(acc_s)

    @pl.when(lacks_low)
    def _():
        kv_s[o, 0, half:, :] = jnp.zeros((half, 2 * kvw), BF16)

    @pl.when(i == 1)
    def _():
        kv_s[o, 1, :half, :] = jnp.zeros((half, 2 * kvw), BF16)

    for h in range(heads):
        for b in range(2):
            q_copy(h, b).wait()

    def low_step(d, carry):
        @pl.when(d < o)
        def _():
            receive_low(d + 1)

        @pl.when(d == jnp.maximum(o - 1, 0))
        def _():
            own_high(begin)

            def early(k, inner):
                for h in range(cuts):
                    receive_above(k, h)
                return inner

            lax.fori_loop(0, jnp.minimum(above, 2), early, 0)

        attend_low(d)
        return carry

    lax.fori_loop(0, o + 1, low_step, 0)

    def next_piece(idx, carry):
        piece(idx)
        return carry

    dense = above >= pieces + 2
    per = (pieces + 1) // 2
    lax.fori_loop(0, jnp.where(above > 2, 0, pieces), next_piece, 0)

    def some_pieces(first, last):
        lax.fori_loop(jnp.clip(first, 0, pieces), jnp.clip(last, 0, pieces), next_piece, 0)

    def high_step(k, carry):
        idx = k - 2
        for h in range(cuts):
            @pl.when(k < above)
            def _():
                receive_above(k, h)

            if h == 0:
                first = jnp.where(dense, idx, jnp.where(above > 2, (k - above) * per, pieces))
                some_pieces(first, first + jnp.where(dense, 1, per))

        def high(x, inner):
            inside = x == 0
            attend_high(jnp.where(inside, o, o + 1 + idx // 2), jnp.where(inside, 1, idx % 2))
            return inner

        lax.fori_loop(jnp.where((idx == 0) & (above > 0), 0, 1), jnp.where(idx < above - 1, 2, 1), high, 0)
        return carry

    lax.fori_loop(2, jnp.maximum(above, 1) + 2, high_step, 0)
    attend_last()
    lax.fori_loop(pieces + 1, 2 * pieces, next_piece, 0)

    for b in range(2):
        for p in range(parts):
            x = n_far + p
            mate_copy(b, x).wait_recv()
            near_ref[b * half:(b + 1) * half, p * chunk:(p + 1) * chunk] = own_s[b, x] + mate_in[b, x].astype(F32)
    for b in range(2):
        for x in range(n_far):
            far_copy(b, x).wait_recv()

    for b in range(2):
        for x in range(pieces):
            mate_copy(b, x).wait_send()
        for x in range(n_far):
            far_copy(b, x).wait_send()

    own_low(finish)
    own_high(finish)
    down(o, 1, finish)

    def drain_low(jo, carry):
        up(jo, finish)
        across(jo, 0, finish)
        return carry

    lax.fori_loop(0, o, drain_low, 0)

    def drain_above(jo, carry):
        for e in range(2):
            down(jo, e, finish)
            across(jo, e, finish)
        return carry

    lax.fori_loop(o + 1, m, drain_above, 0)


def solution(mesh):
    n, t = mesh.shape["ctx"], mesh.shape["tp"]

    def on_device(queries, keys, values, lengths, out_weight):
        rows, width = queries.shape
        half = rows // 2
        kvw = keys.shape[1]
        kvl = kvw // HD
        group = QH // KVH
        heads = width // HD
        feat = out_weight.shape[1] // t
        chunk = min(feat, 512)
        pieces = (t // 2) * (feat // chunk)
        far = max(1, (t // 2 - 1) * (feat // chunk))
        cuts = kvl
        dma = pltpu.SemaphoreType.DMA
        hbm = pl.BlockSpec(memory_space=pl.ANY)
        near, others = pl.pallas_call(
            functools.partial(kernel, n, t, chunk),
            out_shape=[
                pltpu.VMEM((rows, feat), F32),
                pltpu.VMEM((max(1, t // 2 - 1), rows, feat), BF16),
            ],
            in_specs=[pl.BlockSpec(memory_space=pltpu.SMEM), hbm, hbm, hbm, hbm],
            out_specs=[pl.BlockSpec(memory_space=pltpu.VMEM)] * 2,
            scratch_shapes=[
                pltpu.VMEM((2, kvl, group * half, HD), BF16),
                pltpu.VMEM((n // 2, 2, 2 * half, 2 * kvw), BF16),
                pltpu.VMEM(out_weight.shape, BF16),
                pltpu.VMEM((2, kvl, group * half, half), F32),
                pltpu.VMEM((2, kvl, group * half, half), F32),
                pltpu.VMEM((2, kvl, group * half, HD), F32),
                pltpu.VMEM((half, width), BF16),
                pltpu.VMEM((2, pieces, half, chunk), F32),
                pltpu.VMEM((3, half, chunk), F32),
                pltpu.VMEM((2, pieces, half, chunk), BF16),
                pltpu.VMEM((2, pieces, half, chunk), BF16),
                pltpu.VMEM((2, far, half, chunk), BF16),
                dma((heads, 2)),
                dma((2, 2, kvl)),
                dma,
                dma((3, n // 2, 2, cuts)),
                dma((n, 2, cuts)),
                dma((2, pieces)),
                dma((2, pieces)),
                dma((2, far)),
                dma((2, far)),
            ],
            compiler_params=pltpu.CompilerParams(
                collective_id=0, has_side_effects=True, vmem_limit_bytes=56 * 1024 * 1024
            ),
        )(lengths, queries, keys, values, out_weight)
        return (near + jnp.sum(others.astype(F32), axis=0)).astype(BF16)

    return jax.shard_map(
        on_device,
        mesh=mesh,
        in_specs=(P("ctx", "tp"), P("ctx", "tp"), P("ctx", "tp"), P(), P("tp", None)),
        out_specs=P("ctx", "tp"),
        check_vma=False,
    )
```

```python
import functools
import math

import jax
import jax.numpy as jnp
from jax import lax
from jax.experimental import pallas as pl
from jax.experimental.pallas import tpu as pltpu
from jax.sharding import PartitionSpec as P

QH = 64
KVH = 8
HD = 128
NEG = -1e30
MESH = pl.DeviceIdType.MESH
F32 = jnp.float32
BF16 = jnp.bfloat16


def kernel(
    n, t, chunk,
    len_ref, q_hbm, k_hbm, v_hbm, w_hbm,
    near_ref, far_ref,
    q_s, kv_s, w_s, m_s, l_s, acc_s, att_s, own_s, first_s,
    mate_out, mate_in, far_out,
    q_sem, kv_sem, w_sem, send_sem, recv_sem,
    mate_send, mate_recv, far_send, far_recv,
):
    c = lax.axis_index("ctx")
    g = lax.axis_index("tp")
    o, i = c // 2, c % 2
    y, core = g // 2, g % 2
    m = n // 2
    ny = t // 2
    half = q_hbm.shape[0] // 2
    cuts = recv_sem.shape[2]
    kvw = k_hbm.shape[1]
    kvl = kvw // HD
    group = QH // KVH
    heads = kvl * group
    feat = w_hbm.shape[1] // t
    parts = feat // chunk
    factor = HD ** (-0.5) * math.log2(math.e)

    def q_copy(h, b):
        return pltpu.make_async_copy(
            q_hbm.at[pl.ds(b * half, half), pl.ds(h * HD, HD)],
            q_s.at[b, h // group, pl.ds((h % group) * half, half), :],
            q_sem.at[h, b],
        )

    def kv_copy(which, b, h):
        src = k_hbm if which == 0 else v_hbm
        return pltpu.make_async_copy(
            src.at[pl.ds(b * half, half), pl.ds(h * HD, HD)],
            kv_s.at[o, b, pl.ds(i * half, half), pl.ds((2 * h + which) * HD, HD)],
            kv_sem.at[which, b, h],
        )

    own = [(which, b, h) for b in range(2) for h in range(kvl) for which in range(2)]
    for part in own:
        kv_copy(*part).start()
    barrier = pltpu.get_barrier_semaphore()

    def greet(**where):
        pl.semaphore_signal(barrier, inc=1, device_id=where, device_id_type=MESH)

    @pl.when(o + 1 < m)
    def _():
        greet(ctx=c + 2)

    @pl.when(o >= 1)
    def _():
        greet(ctx=c - 2)

    greet(ctx=o * 2 + 1 - i)
    greet(tp=y * 2 + 1 - core)
    for d in range(1, ny):
        greet(tp=((y + d) % ny) * 2 + core)
    w_copy = pltpu.make_async_copy(w_hbm, w_s, w_sem)
    longest = n * half * 2 * 3 // 4
    reach = (longest - 2) // half + 1

    def need_low(jo, target):
        return 2 * n - 1 - target - (2 * jo + 1) <= reach

    lacks_low = (i == 0) & jnp.logical_not(need_low(o, c))

    def kv_piece(direction, jo, e, h):
        target = (c + 2, c - 2, o * 2 + 1 - i)[direction]
        rows = kv_s.at[jo, e, pl.ds(i * half, half), pl.ds(h * 2 * HD, 2 * HD)]
        return pltpu.make_async_remote_copy(
            src_ref=rows,
            dst_ref=rows,
            send_sem=send_sem.at[direction, jo, e, h],
            recv_sem=recv_sem.at[jo * 2 + i, e, h],
            device_id={"ctx": target},
            device_id_type=MESH,
        )

    def kv_arrived(jo, k, e, h):
        rows = kv_s.at[jo, e, pl.ds(k * half, half), pl.ds(h * 2 * HD, 2 * HD)]
        pltpu.make_async_remote_copy(
            src_ref=rows,
            dst_ref=rows,
            send_sem=send_sem.at[0, 0, 0, 0],
            recv_sem=recv_sem.at[jo * 2 + k, e, h],
            device_id={"ctx": o * 2 + 1 - i},
            device_id_type=MESH,
        ).wait_recv()

    def up(jo, act):
        @pl.when(o + 1 < m)
        def _():
            for h in range(cuts):
                act(kv_piece(0, jo, 0, h))

    def down(jo, e, act):
        @pl.when(o >= 1)
        def _():
            for h in range(cuts):
                act(kv_piece(1, jo, e, h))

    def across(jo, e, act):
        for h in range(cuts):
            act(kv_piece(2, jo, e, h))

    mate_lacks_low = (i == 1) & jnp.logical_not(need_low(o, c - 1))
    begin = lambda copy: copy.start()
    finish = lambda copy: copy.wait_send()

    def own_low(act):
        up(o, act)

        @pl.when(jnp.logical_not(mate_lacks_low))
        def _():
            across(o, 0, act)

        down(o, 0, act)

    def own_high(act):
        @pl.when(i == 1)
        def _():
            across(o, 1, act)

    ends = []
    total = jnp.int32(0)
    for d in range(len_ref.shape[0]):
        total = total + len_ref[d]
        ends.append(total)

    def attend(b, jo, e, ready=None, after=None):
        q_first = jnp.where(b == 0, c, 2 * n - 1 - c) * half
        q_place = q_first + lax.broadcasted_iota(jnp.int32, (half, half), 0)
        start = jnp.zeros((half, half), jnp.int32)
        for end in ends:
            start = jnp.where(q_place >= end, end, start)
        biases = []
        for k in range(2):
            block = jnp.where(e == 0, 2 * jo + k, 2 * n - 1 - 2 * jo - k)
            k_place = block * half + lax.broadcasted_iota(jnp.int32, (half, half), 1)
            ok = (k_place >= start) & (k_place <= q_place)
            biases.append(jnp.where(ok, 0.0, NEG).astype(F32))
        for kh in range(kvl):
            if ready is not None:
                ready(kh)
            q = q_s[b, kh]
            key = kv_s[jo, e, :, 2 * kh * HD:(2 * kh + 1) * HD]
            s = lax.dot_general(q, key, (((1,), (1,)), ((), ())), preferred_element_type=F32)
            scores = []
            for k in range(2):
                part = s[:, k * half:(k + 1) * half].reshape(group, half, half) * factor + biases[k][None]
                scores.append(part.reshape(group * half, half))
            m_old = m_s[b, kh]
            m_new = jnp.maximum(m_old, jnp.max(jnp.maximum(*scores), axis=1, keepdims=True))
            alpha = jnp.exp2(m_old - m_new)
            ps = [jnp.exp2(part - m_new) for part in scores]
            m_s[b, kh] = m_new
            l_s[b, kh] = l_s[b, kh] * alpha + (ps[0] + ps[1])
            p = jnp.concatenate([part.astype(BF16) for part in ps], axis=1)
            value = kv_s[jo, e, :, (2 * kh + 1) * HD:(2 * kh + 2) * HD]
            acc_s[b, kh] = acc_s[b, kh] * alpha + jnp.dot(p, value, preferred_element_type=F32)
            if after is not None:
                after(kh)

    n_far = (ny - 1) * parts
    pieces = ny * parts

    def mate_copy(b, x):
        return pltpu.make_async_remote_copy(
            src_ref=mate_out.at[b, x],
            dst_ref=mate_in.at[b, x],
            send_sem=mate_send.at[b, x],
            recv_sem=mate_recv.at[b, x],
            device_id={"tp": y * 2 + 1 - core},
            device_id_type=MESH,
        )

    def far_copy(b, x):
        d = x // parts + 1
        return pltpu.make_async_remote_copy(
            src_ref=far_out.at[b, x],
            dst_ref=far_ref.at[d - 1, pl.ds(b * half, half), pl.ds(pl.multiple_of((x % parts) * chunk, chunk), chunk)],
            send_sem=far_send.at[b, x],
            recv_sem=far_recv.at[b, x],
            device_id={"tp": ((y + d) % ny) * 2 + core},
            device_id_type=MESH,
        )

    def normalize(b, kh):
        inv = 1.0 / jnp.sum(l_s[b, kh], axis=1, keepdims=True)
        done = (acc_s[b, kh] * inv).astype(BF16)
        for r in range(group):
            h = kh * group + r
            att_s[:, h * HD:(h + 1) * HD] = done[r * half:(r + 1) * half]

    span = group * HD

    def first_products(kh):
        normalize(1, kh)
        for number, (x, mine) in enumerate(((0, False), (0, True), (1, False))):
            d = x // parts + 1 if x < n_far else 0
            first = (((y + d) % ny) * 2 + (core if mine else 1 - core)) * feat + (x % parts) * chunk
            cols = pl.ds(pl.multiple_of(first, chunk), chunk)
            rows = slice(kh * span, (kh + 1) * span)
            value = jnp.dot(att_s[:, rows], w_s[rows, cols], preferred_element_type=F32)
            if kh > 0:
                value = value + first_s[number]
            if kh < kvl - 1:
                first_s[number] = value
            elif mine:
                own_s[1, x] = value
            else:
                mate_out[1, x] = value.astype(BF16)
                mate_copy(1, x).start()

    def piece(idx):
        b, x = idx // pieces, idx % pieces

        @pl.when(idx == 0)
        def _():
            w_copy.wait()

        @pl.when(x == 0)
        def _():
            for kh in range(kvl):
                normalize(b, kh)
            first = (((y + jnp.where(n_far > 0, 1, 0)) % ny) * 2 + 1 - core) * feat
            cols = pl.ds(pl.multiple_of(first, chunk), chunk)
            mate_out[b, 0] = jnp.dot(att_s[...], w_s[:, cols], preferred_element_type=F32).astype(BF16)

        d = jnp.where(x < n_far, x // parts + 1, 0)
        p = x % parts

        def term(k):
            first = (((y + d) % ny) * 2 + k) * feat + p * chunk
            cols = pl.ds(pl.multiple_of(first, chunk), chunk)
            return jnp.dot(att_s[...], w_s[:, cols], preferred_element_type=F32)

        @pl.when((x > 0) & (idx != pieces + 1))
        def _():
            mate_out[b, x] = term(1 - core).astype(BF16)

        @pl.when(idx != pieces + 1)
        def _():
            mate_copy(b, x).start()

        @pl.when((x >= 1) & (x <= n_far))
        def _():
            mate_copy(b, x - 1).wait_recv()
            far_out[b, x - 1] = (own_s[b, x - 1] + mate_in[b, x - 1].astype(F32)).astype(BF16)
            far_copy(b, x - 1).start()

        own_s[b, x] = term(core)

    def mate_low(jo):
        for h in range(cuts):
            kv_arrived(jo, 1 - i, 0, h)

    def attend_low(d):
        jo = o - d

        @pl.when((d > 0) | jnp.logical_not(lacks_low))
        def _():
            mate_low(jo)

        def one(b, carry):
            attend(b, jo, 0)
            return carry

        lax.fori_loop(0, jnp.where(need_low(jo, c), 2, 1), one, 0)

    def receive_low(d):
        jo = o - d
        for h in range(cuts):
            kv_arrived(jo, i, 0, h)

            @pl.when(o + 1 < m)
            def _():
                kv_piece(0, jo, 0, h).start()

            kv_piece(2, jo, 0, h).start()

    above = 2 * (m - 1 - o)

    def receive_above(k, h):
        jo, e = o + 1 + k // 2, k % 2
        kv_arrived(jo, i, e, h)

        @pl.when(o >= 1)
        def _():
            kv_piece(1, jo, e, h).start()

        kv_piece(2, jo, e, h).start()

    def attend_high(jo, e):
        @pl.when((jo > o) | (i == 0))
        def _():
            for h in range(cuts):
                kv_arrived(jo, 1 - i, e, h)

        attend(1, jo, e)

    def attend_last():
        jo = jnp.where(above > 0, m - 1, o)

        def ready(kh):
            @pl.when((above > 0) | (i == 0))
            def _():
                kv_arrived(jo, 1 - i, 1, kh)

        attend(1, jo, 1, ready, first_products)

    for part in own:
        kv_copy(*part).wait()
    line = jnp.where(o + 1 < m, 1, 0) + jnp.where(o >= 1, 1, 0)
    pl.semaphore_wait(barrier, line + 1 + ny)
    own_low(begin)
    down(o, 1, begin)
    for h in range(heads):
        for b in range(2):
            q_copy(h, b).start()
    w_copy.start()
    m_s[...] = jnp.full_like(m_s, NEG)
    l_s[...] = jnp.zeros_like(l_s)
    acc_s[...] = jnp.zeros_like(acc_s)

    @pl.when(lacks_low)
    def _():
        kv_s[o, 0, half:, :] = jnp.zeros((half, 2 * kvw), BF16)

    @pl.when(i == 1)
    def _():
        kv_s[o, 1, :half, :] = jnp.zeros((half, 2 * kvw), BF16)

    for h in range(heads):
        for b in range(2):
            q_copy(h, b).wait()

    def low_step(d, carry):
        @pl.when(d < o)
        def _():
            receive_low(d + 1)

        @pl.when(d == jnp.maximum(o - 1, 0))
        def _():
            own_high(begin)

            def early(k, inner):
                for h in range(cuts):
                    receive_above(k, h)
                return inner

            lax.fori_loop(0, jnp.minimum(above, 2), early, 0)

        attend_low(d)
        return carry

    lax.fori_loop(0, o + 1, low_step, 0)

    def next_piece(idx, carry):
        piece(idx)
        return carry

    dense = above >= pieces + 2
    per = (pieces + 1) // 2
    lax.fori_loop(0, jnp.where(above > 2, 0, pieces), next_piece, 0)

    def some_pieces(first, last):
        lax.fori_loop(jnp.clip(first, 0, pieces), jnp.clip(last, 0, pieces), next_piece, 0)

    def high_step(k, carry):
        idx = k - 2
        for h in range(cuts):
            @pl.when(k < above)
            def _():
                receive_above(k, h)

            if h == 0:
                first = jnp.where(dense, idx, jnp.where(above > 2, (k - above) * per, pieces))
                some_pieces(first, first + jnp.where(dense, 1, per))

        def high(x, inner):
            inside = x == 0
            attend_high(jnp.where(inside, o, o + 1 + turn // 2), jnp.where(inside, 1, turn % 2))
            return inner

        turn = idx - 1
        inner = (turn >= 0) & (turn < above - 1)
        lax.fori_loop(jnp.where((idx == 0) & (above > 0), 0, 1), jnp.where(inner, 2, 1), high, 0)
        return carry

    lax.fori_loop(2, jnp.maximum(above, 1) + 2, high_step, 0)
    attend_last()
    lax.fori_loop(pieces + 1, 2 * pieces, next_piece, 0)

    for b in range(2):
        for p in range(parts):
            x = n_far + p
            mate_copy(b, x).wait_recv()
            near_ref[b * half:(b + 1) * half, p * chunk:(p + 1) * chunk] = own_s[b, x] + mate_in[b, x].astype(F32)

    for b in range(2):
        for x in range(pieces):
            mate_copy(b, x).wait_send()

    own_low(finish)
    own_high(finish)
    down(o, 1, finish)

    def drain_low(jo, carry):
        up(jo, finish)
        across(jo, 0, finish)
        return carry

    lax.fori_loop(0, o, drain_low, 0)

    def drain_above(jo, carry):
        for e in range(2):
            down(jo, e, finish)
            across(jo, e, finish)
        return carry

    lax.fori_loop(o + 1, m, drain_above, 0)

    for b in range(2):
        for x in range(n_far):
            far_copy(b, x).wait_send()
    for b in range(2):
        for x in range(n_far):
            far_copy(b, x).wait_recv()


def solution(mesh):
    n, t = mesh.shape["ctx"], mesh.shape["tp"]

    def on_device(queries, keys, values, lengths, out_weight):
        rows, width = queries.shape
        half = rows // 2
        kvw = keys.shape[1]
        kvl = kvw // HD
        group = QH // KVH
        heads = width // HD
        feat = out_weight.shape[1] // t
        chunk = min(feat, 512)
        pieces = (t // 2) * (feat // chunk)
        far = max(1, (t // 2 - 1) * (feat // chunk))
        cuts = kvl
        dma = pltpu.SemaphoreType.DMA
        hbm = pl.BlockSpec(memory_space=pl.ANY)
        near, others = pl.pallas_call(
            functools.partial(kernel, n, t, chunk),
            out_shape=[
                pltpu.VMEM((rows, feat), F32),
                pltpu.VMEM((max(1, t // 2 - 1), rows, feat), BF16),
            ],
            in_specs=[pl.BlockSpec(memory_space=pltpu.SMEM), hbm, hbm, hbm, hbm],
            out_specs=[pl.BlockSpec(memory_space=pltpu.VMEM)] * 2,
            scratch_shapes=[
                pltpu.VMEM((2, kvl, group * half, HD), BF16),
                pltpu.VMEM((n // 2, 2, 2 * half, 2 * kvw), BF16),
                pltpu.VMEM(out_weight.shape, BF16),
                pltpu.VMEM((2, kvl, group * half, half), F32),
                pltpu.VMEM((2, kvl, group * half, half), F32),
                pltpu.VMEM((2, kvl, group * half, HD), F32),
                pltpu.VMEM((half, width), BF16),
                pltpu.VMEM((2, pieces, half, chunk), F32),
                pltpu.VMEM((3, half, chunk), F32),
                pltpu.VMEM((2, pieces, half, chunk), BF16),
                pltpu.VMEM((2, pieces, half, chunk), BF16),
                pltpu.VMEM((2, far, half, chunk), BF16),
                dma((heads, 2)),
                dma((2, 2, kvl)),
                dma,
                dma((3, n // 2, 2, cuts)),
                dma((n, 2, cuts)),
                dma((2, pieces)),
                dma((2, pieces)),
                dma((2, far)),
                dma((2, far)),
            ],
            compiler_params=pltpu.CompilerParams(
                collective_id=0, has_side_effects=True, vmem_limit_bytes=56 * 1024 * 1024
            ),
        )(lengths, queries, keys, values, out_weight)
        return (near + jnp.sum(others.astype(F32), axis=0)).astype(BF16)

    return jax.shard_map(
        on_device,
        mesh=mesh,
        in_specs=(P("ctx", "tp"), P("ctx", "tp"), P("ctx", "tp"), P(), P("tp", None)),
        out_specs=P("ctx", "tp"),
        check_vma=False,
    )
```

```python
import functools
import math

import jax
import jax.numpy as jnp
from jax import lax
from jax.experimental import pallas as pl
from jax.experimental.pallas import tpu as pltpu
from jax.sharding import PartitionSpec as P

QH = 64
KVH = 8
HD = 128
NEG = -1e30
MESH = pl.DeviceIdType.MESH
F32 = jnp.float32
BF16 = jnp.bfloat16


def kernel(
    n, t, chunk,
    len_ref, q_hbm, k_hbm, v_hbm, w_hbm,
    near_ref, far_ref,
    q_s, kv_s, w_s, m_s, l_s, acc_s, att_s, own_s, first_s,
    mate_out, mate_in, far_out,
    q_sem, kv_sem, w_sem, send_sem, recv_sem,
    mate_send, mate_recv, far_send, far_recv,
):
    c = lax.axis_index("ctx")
    g = lax.axis_index("tp")
    o, i = c // 2, c % 2
    y, core = g // 2, g % 2
    m = n // 2
    ny = t // 2
    half = q_hbm.shape[0] // 2
    cuts = recv_sem.shape[2]
    kvw = k_hbm.shape[1]
    kvl = kvw // HD
    group = QH // KVH
    heads = kvl * group
    feat = w_hbm.shape[1] // t
    parts = feat // chunk
    factor = HD ** (-0.5) * math.log2(math.e)

    def q_copy(h, b):
        return pltpu.make_async_copy(
            q_hbm.at[pl.ds(b * half, half), pl.ds(h * HD, HD)],
            q_s.at[b, h // group, pl.ds((h % group) * half, half), :],
            q_sem.at[h, b],
        )

    def kv_copy(which, b, h):
        src = k_hbm if which == 0 else v_hbm
        return pltpu.make_async_copy(
            src.at[pl.ds(b * half, half), pl.ds(h * HD, HD)],
            kv_s.at[o, b, pl.ds(i * half, half), pl.ds((2 * h + which) * HD, HD)],
            kv_sem.at[which, b, h],
        )

    own = [(which, b, h) for b in range(2) for h in range(kvl) for which in range(2)]
    for part in own:
        kv_copy(*part).start()
    barrier = pltpu.get_barrier_semaphore()

    def greet(**where):
        pl.semaphore_signal(barrier, inc=1, device_id=where, device_id_type=MESH)

    @pl.when(o + 1 < m)
    def _():
        greet(ctx=c + 2)

    @pl.when(o >= 1)
    def _():
        greet(ctx=c - 2)

    greet(ctx=o * 2 + 1 - i)
    greet(tp=y * 2 + 1 - core)
    for d in range(1, ny):
        greet(tp=((y + d) % ny) * 2 + core)
    w_copy = pltpu.make_async_copy(w_hbm, w_s, w_sem)
    longest = n * half * 2 * 3 // 4
    reach = (longest - 2) // half + 1

    def need_low(jo, target):
        return 2 * n - 1 - target - (2 * jo + 1) <= reach

    lacks_low = (i == 0) & jnp.logical_not(need_low(o, c))

    def kv_piece(direction, jo, e, h):
        target = (c + 2, c - 2, o * 2 + 1 - i)[direction]
        rows = kv_s.at[jo, e, pl.ds(i * half, half), pl.ds(h * 2 * HD, 2 * HD)]
        return pltpu.make_async_remote_copy(
            src_ref=rows,
            dst_ref=rows,
            send_sem=send_sem.at[direction, jo, e, h],
            recv_sem=recv_sem.at[jo * 2 + i, e, h],
            device_id={"ctx": target},
            device_id_type=MESH,
        )

    def kv_arrived(jo, k, e, h):
        rows = kv_s.at[jo, e, pl.ds(k * half, half), pl.ds(h * 2 * HD, 2 * HD)]
        pltpu.make_async_remote_copy(
            src_ref=rows,
            dst_ref=rows,
            send_sem=send_sem.at[0, 0, 0, 0],
            recv_sem=recv_sem.at[jo * 2 + k, e, h],
            device_id={"ctx": o * 2 + 1 - i},
            device_id_type=MESH,
        ).wait_recv()

    def up(jo, act):
        @pl.when(o + 1 < m)
        def _():
            for h in range(cuts):
                act(kv_piece(0, jo, 0, h))

    def down(jo, e, act):
        @pl.when(o >= 1)
        def _():
            for h in range(cuts):
                act(kv_piece(1, jo, e, h))

    def across(jo, e, act):
        for h in range(cuts):
            act(kv_piece(2, jo, e, h))

    mate_lacks_low = (i == 1) & jnp.logical_not(need_low(o, c - 1))
    begin = lambda copy: copy.start()
    finish = lambda copy: copy.wait_send()

    def own_low(act):
        up(o, act)

        @pl.when(jnp.logical_not(mate_lacks_low))
        def _():
            across(o, 0, act)

        down(o, 0, act)

    def own_high(act):
        @pl.when(i == 1)
        def _():
            across(o, 1, act)

    ends = []
    total = jnp.int32(0)
    for d in range(len_ref.shape[0]):
        total = total + len_ref[d]
        ends.append(total)

    def attend(b, jo, e, ready=None, after=None):
        q_first = jnp.where(b == 0, c, 2 * n - 1 - c) * half
        q_place = q_first + lax.broadcasted_iota(jnp.int32, (half, half), 0)
        start = jnp.zeros((half, half), jnp.int32)
        for end in ends:
            start = jnp.where(q_place >= end, end, start)
        biases = []
        for k in range(2):
            block = jnp.where(e == 0, 2 * jo + k, 2 * n - 1 - 2 * jo - k)
            k_place = block * half + lax.broadcasted_iota(jnp.int32, (half, half), 1)
            ok = (k_place >= start) & (k_place <= q_place)
            biases.append(jnp.where(ok, 0.0, NEG).astype(F32))
        for kh in range(kvl):
            if ready is not None:
                ready(kh)
            q = q_s[b, kh]
            key = kv_s[jo, e, :, 2 * kh * HD:(2 * kh + 1) * HD]
            s = lax.dot_general(q, key, (((1,), (1,)), ((), ())), preferred_element_type=F32)
            scores = []
            for k in range(2):
                part = s[:, k * half:(k + 1) * half].reshape(group, half, half) * factor + biases[k][None]
                scores.append(part.reshape(group * half, half))
            m_old = m_s[b, kh]
            m_new = jnp.maximum(m_old, jnp.max(jnp.maximum(*scores), axis=1, keepdims=True))
            alpha = jnp.exp2(m_old - m_new)
            ps = [jnp.exp2(part - m_new) for part in scores]
            m_s[b, kh] = m_new
            l_s[b, kh] = l_s[b, kh] * alpha + (ps[0] + ps[1])
            p = jnp.concatenate([part.astype(BF16) for part in ps], axis=1)
            value = kv_s[jo, e, :, (2 * kh + 1) * HD:(2 * kh + 2) * HD]
            acc_s[b, kh] = acc_s[b, kh] * alpha + jnp.dot(p, value, preferred_element_type=F32)
            if after is not None:
                after(kh)

    n_far = (ny - 1) * parts
    pieces = ny * parts

    def mate_copy(b, x):
        return pltpu.make_async_remote_copy(
            src_ref=mate_out.at[b, x],
            dst_ref=mate_in.at[b, x],
            send_sem=mate_send.at[b, x],
            recv_sem=mate_recv.at[b, x],
            device_id={"tp": y * 2 + 1 - core},
            device_id_type=MESH,
        )

    def far_copy(b, x):
        d = x // parts + 1
        return pltpu.make_async_remote_copy(
            src_ref=far_out.at[b, x],
            dst_ref=far_ref.at[d - 1, pl.ds(b * half, half), pl.ds(pl.multiple_of((x % parts) * chunk, chunk), chunk)],
            send_sem=far_send.at[b, x],
            recv_sem=far_recv.at[b, x],
            device_id={"tp": ((y + d) % ny) * 2 + core},
            device_id_type=MESH,
        )

    def normalize(b, kh):
        inv = 1.0 / jnp.sum(l_s[b, kh], axis=1, keepdims=True)
        done = (acc_s[b, kh] * inv).astype(BF16)
        for r in range(group):
            h = kh * group + r
            att_s[:, h * HD:(h + 1) * HD] = done[r * half:(r + 1) * half]

    span = group * HD

    def first_products(kh):
        normalize(1, kh)
        for number, (x, mine) in enumerate(((0, False), (0, True), (1, False))):
            d = x // parts + 1 if x < n_far else 0
            first = (((y + d) % ny) * 2 + (core if mine else 1 - core)) * feat + (x % parts) * chunk
            cols = pl.ds(pl.multiple_of(first, chunk), chunk)
            rows = slice(kh * span, (kh + 1) * span)
            value = jnp.dot(att_s[:, rows], w_s[rows, cols], preferred_element_type=F32)
            if kh > 0:
                value = value + first_s[number]
            if kh < kvl - 1:
                first_s[number] = value
            elif mine:
                own_s[1, x] = value
            else:
                mate_out[1, x] = value.astype(BF16)
                mate_copy(1, x).start()

    def piece(idx):
        b, x = idx // pieces, idx % pieces

        @pl.when(idx == 0)
        def _():
            w_copy.wait()

        @pl.when(x == 0)
        def _():
            for kh in range(kvl):
                normalize(b, kh)
            first = (((y + jnp.where(n_far > 0, 1, 0)) % ny) * 2 + 1 - core) * feat
            cols = pl.ds(pl.multiple_of(first, chunk), chunk)
            mate_out[b, 0] = jnp.dot(att_s[...], w_s[:, cols], preferred_element_type=F32).astype(BF16)

        d = jnp.where(x < n_far, x // parts + 1, 0)
        p = x % parts

        def term(k):
            first = (((y + d) % ny) * 2 + k) * feat + p * chunk
            cols = pl.ds(pl.multiple_of(first, chunk), chunk)
            return jnp.dot(att_s[...], w_s[:, cols], preferred_element_type=F32)

        @pl.when((x > 0) & (idx != pieces + 1))
        def _():
            mate_out[b, x] = term(1 - core).astype(BF16)

        @pl.when(idx != pieces + 1)
        def _():
            mate_copy(b, x).start()

        @pl.when((x >= 1) & (x <= n_far))
        def _():
            mate_copy(b, x - 1).wait_recv()
            far_out[b, x - 1] = (own_s[b, x - 1] + mate_in[b, x - 1].astype(F32)).astype(BF16)
            far_copy(b, x - 1).start()

        own_s[b, x] = term(core)

    def mate_low(jo):
        for h in range(cuts):
            kv_arrived(jo, 1 - i, 0, h)

    def attend_low(d):
        jo = o - d

        @pl.when((d > 0) | jnp.logical_not(lacks_low))
        def _():
            mate_low(jo)

        def one(b, carry):
            attend(b, jo, 0)
            return carry

        lax.fori_loop(0, jnp.where(need_low(jo, c), 2, 1), one, 0)

    def receive_low(d):
        jo = o - d
        for h in range(cuts):
            kv_arrived(jo, i, 0, h)

            @pl.when(o + 1 < m)
            def _():
                kv_piece(0, jo, 0, h).start()

            kv_piece(2, jo, 0, h).start()

    above = 2 * (m - 1 - o)

    def receive_above(k, h):
        jo, e = o + 1 + k // 2, k % 2
        kv_arrived(jo, i, e, h)
        kv_piece(2, jo, e, h).start()

        @pl.when(o >= 1)
        def _():
            kv_piece(1, jo, e, h).start()

    def attend_high(jo, e):
        @pl.when((jo > o) | (i == 0))
        def _():
            for h in range(cuts):
                kv_arrived(jo, 1 - i, e, h)

        attend(1, jo, e)

    def attend_last():
        jo = jnp.where(above > 0, m - 1, o)

        def ready(kh):
            @pl.when((above > 0) | (i == 0))
            def _():
                kv_arrived(jo, 1 - i, 1, kh)

        attend(1, jo, 1, ready, first_products)

    for part in own:
        kv_copy(*part).wait()
    line = jnp.where(o + 1 < m, 1, 0) + jnp.where(o >= 1, 1, 0)
    pl.semaphore_wait(barrier, line + 1 + ny)
    own_low(begin)
    down(o, 1, begin)
    m_s[...] = jnp.full_like(m_s, NEG)
    l_s[...] = jnp.zeros_like(l_s)
    acc_s[...] = jnp.zeros_like(acc_s)

    for h in range(heads):
        for b in range(2):
            q_copy(h, b).start()
    w_copy.start()
    @pl.when(lacks_low)
    def _():
        kv_s[o, 0, half:, :] = jnp.zeros((half, 2 * kvw), BF16)

    @pl.when(i == 1)
    def _():
        kv_s[o, 1, :half, :] = jnp.zeros((half, 2 * kvw), BF16)

    for h in range(heads):
        for b in range(2):
            q_copy(h, b).wait()

    def low_step(d, carry):
        @pl.when(d < o)
        def _():
            receive_low(d + 1)

        @pl.when(d == jnp.maximum(o - 1, 0))
        def _():
            own_high(begin)

            def early(k, inner):
                for h in range(cuts):
                    receive_above(k, h)
                return inner

            lax.fori_loop(0, jnp.minimum(above, 2), early, 0)

        attend_low(d)
        return carry

    lax.fori_loop(0, o + 1, low_step, 0)

    def next_piece(idx, carry):
        piece(idx)
        return carry

    dense = above >= pieces + 2
    per = (pieces + 1) // 2
    lax.fori_loop(0, jnp.where(above > 2, 0, pieces), next_piece, 0)

    def some_pieces(first, last):
        lax.fori_loop(jnp.clip(first, 0, pieces), jnp.clip(last, 0, pieces), next_piece, 0)

    def high_step(k, carry):
        idx = k - 2
        for h in range(cuts):
            @pl.when(k < above)
            def _():
                receive_above(k, h)

            if h == 0:
                first = jnp.where(dense, idx, jnp.where(above > 2, (k - above) * per, pieces))
                some_pieces(first, first + jnp.where(dense, 1, per))

        def high(x, inner):
            inside = x == 0
            attend_high(jnp.where(inside, o, o + 1 + turn // 2), jnp.where(inside, 1, turn % 2))
            return inner

        turn = idx - 1
        inner = (turn >= 0) & (turn < above - 1)
        lax.fori_loop(jnp.where((idx == 0) & (above > 0), 0, 1), jnp.where(inner, 2, 1), high, 0)
        return carry

    lax.fori_loop(2, jnp.maximum(above, 1) + 2, high_step, 0)
    def near_sums(b):
        for p in range(parts):
            x = n_far + p
            mate_copy(b, x).wait_recv()
            near_ref[b * half:(b + 1) * half, p * chunk:(p + 1) * chunk] = own_s[b, x] + mate_in[b, x].astype(F32)

    near_sums(0)
    attend_last()
    lax.fori_loop(pieces + 1, 2 * pieces, next_piece, 0)
    near_sums(1)


    for b in range(2):
        for x in range(pieces):
            mate_copy(b, x).wait_send()

    own_low(finish)
    own_high(finish)
    down(o, 1, finish)

    def drain_low(jo, carry):
        up(jo, finish)
        across(jo, 0, finish)
        return carry

    lax.fori_loop(0, o, drain_low, 0)

    def drain_above(jo, carry):
        for e in range(2):
            down(jo, e, finish)
            across(jo, e, finish)
        return carry

    lax.fori_loop(o + 1, m, drain_above, 0)

    for b in range(2):
        for x in range(n_far):
            far_copy(b, x).wait_send()
    for b in range(2):
        for x in range(n_far):
            far_copy(b, x).wait_recv()


def solution(mesh):
    n, t = mesh.shape["ctx"], mesh.shape["tp"]

    def on_device(queries, keys, values, lengths, out_weight):
        rows, width = queries.shape
        half = rows // 2
        kvw = keys.shape[1]
        kvl = kvw // HD
        group = QH // KVH
        heads = width // HD
        feat = out_weight.shape[1] // t
        chunk = min(feat, 512)
        pieces = (t // 2) * (feat // chunk)
        far = max(1, (t // 2 - 1) * (feat // chunk))
        cuts = kvl
        dma = pltpu.SemaphoreType.DMA
        hbm = pl.BlockSpec(memory_space=pl.ANY)
        near, others = pl.pallas_call(
            functools.partial(kernel, n, t, chunk),
            out_shape=[
                pltpu.VMEM((rows, feat), F32),
                pltpu.VMEM((max(1, t // 2 - 1), rows, feat), BF16),
            ],
            in_specs=[pl.BlockSpec(memory_space=pltpu.SMEM), hbm, hbm, hbm, hbm],
            out_specs=[pl.BlockSpec(memory_space=pltpu.VMEM)] * 2,
            scratch_shapes=[
                pltpu.VMEM((2, kvl, group * half, HD), BF16),
                pltpu.VMEM((n // 2, 2, 2 * half, 2 * kvw), BF16),
                pltpu.VMEM(out_weight.shape, BF16),
                pltpu.VMEM((2, kvl, group * half, half), F32),
                pltpu.VMEM((2, kvl, group * half, half), F32),
                pltpu.VMEM((2, kvl, group * half, HD), F32),
                pltpu.VMEM((half, width), BF16),
                pltpu.VMEM((2, pieces, half, chunk), F32),
                pltpu.VMEM((3, half, chunk), F32),
                pltpu.VMEM((2, pieces, half, chunk), BF16),
                pltpu.VMEM((2, pieces, half, chunk), BF16),
                pltpu.VMEM((2, far, half, chunk), BF16),
                dma((heads, 2)),
                dma((2, 2, kvl)),
                dma,
                dma((3, n // 2, 2, cuts)),
                dma((n, 2, cuts)),
                dma((2, pieces)),
                dma((2, pieces)),
                dma((2, far)),
                dma((2, far)),
            ],
            compiler_params=pltpu.CompilerParams(
                collective_id=0, has_side_effects=True, vmem_limit_bytes=56 * 1024 * 1024
            ),
        )(lengths, queries, keys, values, out_weight)
        return (near + jnp.sum(others.astype(F32), axis=0)).astype(BF16)

    return jax.shard_map(
        on_device,
        mesh=mesh,
        in_specs=(P("ctx", "tp"), P("ctx", "tp"), P("ctx", "tp"), P(), P("tp", None)),
        out_specs=P("ctx", "tp"),
        check_vma=False,
    )
```

```python
import functools
import math

import jax
import jax.numpy as jnp
from jax import lax
from jax.experimental import pallas as pl
from jax.experimental.pallas import tpu as pltpu
from jax.sharding import PartitionSpec as P

QH = 64
KVH = 8
HD = 128
NEG = -1e30
MESH = pl.DeviceIdType.MESH
F32 = jnp.float32
BF16 = jnp.bfloat16


def kernel(
    n, t, chunk,
    len_ref, q_hbm, k_hbm, v_hbm, w_hbm,
    near_ref, far_ref,
    q_s, kv_s, w_s, m_s, l_s, acc_s, att_s, own_s, first_s,
    mate_out, mate_in, far_out,
    q_sem, kv_sem, w_sem, send_sem, recv_sem,
    mate_send, mate_recv, far_send, far_recv,
):
    c = lax.axis_index("ctx")
    g = lax.axis_index("tp")
    o, i = c // 2, c % 2
    y, core = g // 2, g % 2
    m = n // 2
    ny = t // 2
    half = q_hbm.shape[0] // 2
    cuts = recv_sem.shape[2]
    kvw = k_hbm.shape[1]
    kvl = kvw // HD
    group = QH // KVH
    heads = kvl * group
    feat = w_hbm.shape[1] // t
    parts = feat // chunk
    factor = HD ** (-0.5) * math.log2(math.e)

    def q_copy(h, b):
        return pltpu.make_async_copy(
            q_hbm.at[pl.ds(b * half, half), pl.ds(h * HD, HD)],
            q_s.at[b, h // group, pl.ds((h % group) * half, half), :],
            q_sem.at[h, b],
        )

    def kv_copy(which, b, h):
        src = k_hbm if which == 0 else v_hbm
        return pltpu.make_async_copy(
            src.at[pl.ds(b * half, half), pl.ds(h * HD, HD)],
            kv_s.at[o, b, pl.ds(i * half, half), pl.ds((2 * h + which) * HD, HD)],
            kv_sem.at[which, b, h],
        )

    own = [(which, b, h) for b in range(2) for h in range(kvl) for which in range(2)]
    for part in own:
        kv_copy(*part).start()
    barrier = pltpu.get_barrier_semaphore()

    def greet(**where):
        pl.semaphore_signal(barrier, inc=1, device_id=where, device_id_type=MESH)

    @pl.when(o + 1 < m)
    def _():
        greet(ctx=c + 2)

    @pl.when(o >= 1)
    def _():
        greet(ctx=c - 2)

    greet(ctx=o * 2 + 1 - i)
    greet(tp=y * 2 + 1 - core)
    for d in range(1, ny):
        greet(tp=((y + d) % ny) * 2 + core)
    w_copy = pltpu.make_async_copy(w_hbm, w_s, w_sem)
    longest = n * half * 2 * 3 // 4
    reach = (longest - 2) // half + 1

    def need_low(jo, target):
        return 2 * n - 1 - target - (2 * jo + 1) <= reach

    lacks_low = (i == 0) & jnp.logical_not(need_low(o, c))

    def kv_piece(direction, jo, e, h):
        target = (c + 2, c - 2, o * 2 + 1 - i)[direction]
        rows = kv_s.at[jo, e, pl.ds(i * half, half), pl.ds(h * 2 * HD, 2 * HD)]
        return pltpu.make_async_remote_copy(
            src_ref=rows,
            dst_ref=rows,
            send_sem=send_sem.at[direction, jo, e, h],
            recv_sem=recv_sem.at[jo * 2 + i, e, h],
            device_id={"ctx": target},
            device_id_type=MESH,
        )

    def kv_arrived(jo, k, e, h):
        rows = kv_s.at[jo, e, pl.ds(k * half, half), pl.ds(h * 2 * HD, 2 * HD)]
        pltpu.make_async_remote_copy(
            src_ref=rows,
            dst_ref=rows,
            send_sem=send_sem.at[0, 0, 0, 0],
            recv_sem=recv_sem.at[jo * 2 + k, e, h],
            device_id={"ctx": o * 2 + 1 - i},
            device_id_type=MESH,
        ).wait_recv()

    def up(jo, act):
        @pl.when(o + 1 < m)
        def _():
            for h in range(cuts):
                act(kv_piece(0, jo, 0, h))

    def down(jo, e, act):
        @pl.when(o >= 1)
        def _():
            for h in range(cuts):
                act(kv_piece(1, jo, e, h))

    def across(jo, e, act):
        for h in range(cuts):
            act(kv_piece(2, jo, e, h))

    mate_lacks_low = (i == 1) & jnp.logical_not(need_low(o, c - 1))
    begin = lambda copy: copy.start()
    finish = lambda copy: copy.wait_send()

    def own_low(act):
        up(o, act)

        @pl.when(jnp.logical_not(mate_lacks_low))
        def _():
            across(o, 0, act)

        down(o, 0, act)

    def own_high(act):
        @pl.when(i == 1)
        def _():
            across(o, 1, act)

    ends = []
    total = jnp.int32(0)
    for d in range(len_ref.shape[0]):
        total = total + len_ref[d]
        ends.append(total)

    def attend(b, jo, e, ready=None, after=None):
        q_first = jnp.where(b == 0, c, 2 * n - 1 - c) * half
        q_place = q_first + lax.broadcasted_iota(jnp.int32, (half, half), 0)
        start = jnp.zeros((half, half), jnp.int32)
        for end in ends:
            start = jnp.where(q_place >= end, end, start)
        biases = []
        for k in range(2):
            block = jnp.where(e == 0, 2 * jo + k, 2 * n - 1 - 2 * jo - k)
            k_place = block * half + lax.broadcasted_iota(jnp.int32, (half, half), 1)
            ok = (k_place >= start) & (k_place <= q_place)
            biases.append(jnp.where(ok, 0.0, NEG).astype(F32))
        for kh in range(kvl):
            if ready is not None:
                ready(kh)
            q = q_s[b, kh]
            key = kv_s[jo, e, :, 2 * kh * HD:(2 * kh + 1) * HD]
            s = lax.dot_general(q, key, (((1,), (1,)), ((), ())), preferred_element_type=F32)
            scores = []
            for k in range(2):
                part = s[:, k * half:(k + 1) * half].reshape(group, half, half) * factor + biases[k][None]
                scores.append(part.reshape(group * half, half))
            m_old = m_s[b, kh]
            m_new = jnp.maximum(m_old, jnp.max(jnp.maximum(*scores), axis=1, keepdims=True))
            alpha = jnp.exp2(m_old - m_new)
            ps = [jnp.exp2(part - m_new) for part in scores]
            m_s[b, kh] = m_new
            l_s[b, kh] = l_s[b, kh] * alpha + (ps[0] + ps[1])
            p = jnp.concatenate([part.astype(BF16) for part in ps], axis=1)
            value = kv_s[jo, e, :, (2 * kh + 1) * HD:(2 * kh + 2) * HD]
            acc_s[b, kh] = acc_s[b, kh] * alpha + jnp.dot(p, value, preferred_element_type=F32)
            if after is not None:
                after(kh)

    n_far = (ny - 1) * parts
    pieces = ny * parts

    def mate_copy(b, x):
        return pltpu.make_async_remote_copy(
            src_ref=mate_out.at[b, x],
            dst_ref=mate_in.at[b, x],
            send_sem=mate_send.at[b, x],
            recv_sem=mate_recv.at[b, x],
            device_id={"tp": y * 2 + 1 - core},
            device_id_type=MESH,
        )

    def far_copy(b, x):
        d = x // parts + 1
        return pltpu.make_async_remote_copy(
            src_ref=far_out.at[b, x],
            dst_ref=far_ref.at[d - 1, pl.ds(b * half, half), pl.ds(pl.multiple_of((x % parts) * chunk, chunk), chunk)],
            send_sem=far_send.at[b, x],
            recv_sem=far_recv.at[b, x],
            device_id={"tp": ((y + d) % ny) * 2 + core},
            device_id_type=MESH,
        )

    def normalize(b, kh):
        inv = 1.0 / jnp.sum(l_s[b, kh], axis=1, keepdims=True)
        done = (acc_s[b, kh] * inv).astype(BF16)
        for r in range(group):
            h = kh * group + r
            att_s[:, h * HD:(h + 1) * HD] = done[r * half:(r + 1) * half]

    span = group * HD

    def first_products(kh):
        normalize(1, kh)
        for number, (x, mine) in enumerate(((0, False), (0, True), (1, False))):
            d = x // parts + 1 if x < n_far else 0
            first = (((y + d) % ny) * 2 + (core if mine else 1 - core)) * feat + (x % parts) * chunk
            cols = pl.ds(pl.multiple_of(first, chunk), chunk)
            rows = slice(kh * span, (kh + 1) * span)
            value = jnp.dot(att_s[:, rows], w_s[rows, cols], preferred_element_type=F32)
            if kh > 0:
                value = value + first_s[number]
            if kh < kvl - 1:
                first_s[number] = value
            elif mine:
                own_s[1, x] = value
            else:
                mate_out[1, x] = value.astype(BF16)
                mate_copy(1, x).start()

    def piece(idx):
        b, x = idx // pieces, idx % pieces

        @pl.when(idx == 0)
        def _():
            w_copy.wait()

        @pl.when(x == 0)
        def _():
            for kh in range(kvl):
                normalize(b, kh)
            first = (((y + jnp.where(n_far > 0, 1, 0)) % ny) * 2 + 1 - core) * feat
            cols = pl.ds(pl.multiple_of(first, chunk), chunk)
            mate_out[b, 0] = jnp.dot(att_s[...], w_s[:, cols], preferred_element_type=F32).astype(BF16)

        d = jnp.where(x < n_far, x // parts + 1, 0)
        p = x % parts

        def term(k):
            first = (((y + d) % ny) * 2 + k) * feat + p * chunk
            cols = pl.ds(pl.multiple_of(first, chunk), chunk)
            return jnp.dot(att_s[...], w_s[:, cols], preferred_element_type=F32)

        @pl.when((x > 0) & (idx != pieces + 1))
        def _():
            mate_out[b, x] = term(1 - core).astype(BF16)

        @pl.when(idx != pieces + 1)
        def _():
            mate_copy(b, x).start()

        @pl.when((x >= 1) & (x <= n_far))
        def _():
            mate_copy(b, x - 1).wait_recv()
            far_out[b, x - 1] = (own_s[b, x - 1] + mate_in[b, x - 1].astype(F32)).astype(BF16)
            far_copy(b, x - 1).start()

        own_s[b, x] = term(core)

    def mate_low(jo):
        for h in range(cuts):
            kv_arrived(jo, 1 - i, 0, h)

    def attend_low(d):
        jo = o - d

        @pl.when((d > 0) | jnp.logical_not(lacks_low))
        def _():
            mate_low(jo)

        def one(b, carry):
            attend(b, jo, 0)
            return carry

        lax.fori_loop(0, jnp.where(need_low(jo, c), 2, 1), one, 0)

    def receive_low(d):
        jo = o - d
        for h in range(cuts):
            kv_arrived(jo, i, 0, h)

            @pl.when(o + 1 < m)
            def _():
                kv_piece(0, jo, 0, h).start()

            kv_piece(2, jo, 0, h).start()

    above = 2 * (m - 1 - o)

    def receive_above(k, h):
        jo, e = o + 1 + k // 2, k % 2
        kv_arrived(jo, i, e, h)
        kv_piece(2, jo, e, h).start()

        @pl.when(o >= 1)
        def _():
            kv_piece(1, jo, e, h).start()

    def attend_high(jo, e):
        @pl.when((jo > o) | (i == 0))
        def _():
            for h in range(cuts):
                kv_arrived(jo, 1 - i, e, h)

        attend(1, jo, e)

    def attend_last():
        jo = jnp.where(above > 0, m - 1, o)

        def ready(kh):
            @pl.when((above > 0) | (i == 0))
            def _():
                kv_arrived(jo, 1 - i, 1, kh)

        attend(1, jo, 1, ready, first_products)

    for part in own:
        kv_copy(*part).wait()
    line = jnp.where(o + 1 < m, 1, 0) + jnp.where(o >= 1, 1, 0)
    pl.semaphore_wait(barrier, line + 1 + ny)
    own_low(begin)
    down(o, 1, begin)
    m_s[...] = jnp.full_like(m_s, NEG)
    l_s[...] = jnp.zeros_like(l_s)
    acc_s[...] = jnp.zeros_like(acc_s)

    for h in range(heads):
        for b in range(2):
            q_copy(h, b).start()
    w_copy.start()
    @pl.when(lacks_low)
    def _():
        kv_s[o, 0, half:, :] = jnp.zeros((half, 2 * kvw), BF16)

    @pl.when(i == 1)
    def _():
        kv_s[o, 1, :half, :] = jnp.zeros((half, 2 * kvw), BF16)

    for h in range(heads):
        for b in range(2):
            q_copy(h, b).wait()

    def low_step(d, carry):
        @pl.when(d < o)
        def _():
            receive_low(d + 1)

        @pl.when(d == jnp.maximum(o - 1, 0))
        def _():
            own_high(begin)

            def early(k, inner):
                for h in range(cuts):
                    receive_above(k, h)
                return inner

            lax.fori_loop(0, jnp.minimum(above, jnp.where(o == 0, 1, 2)), early, 0)

        attend_low(d)
        return carry

    lax.fori_loop(0, o + 1, low_step, 0)

    @pl.when((o == 0) & (above > 1))
    def _():
        for h in range(cuts):
            receive_above(1, h)

    def next_piece(idx, carry):
        piece(idx)
        return carry

    dense = above >= pieces + 2
    per = (pieces + 1) // 2
    lax.fori_loop(0, jnp.where(above > 2, 0, pieces), next_piece, 0)

    def some_pieces(first, last):
        lax.fori_loop(jnp.clip(first, 0, pieces), jnp.clip(last, 0, pieces), next_piece, 0)

    def high_step(k, carry):
        idx = k - 2
        for h in range(cuts):
            @pl.when(k < above)
            def _():
                receive_above(k, h)

            if h == 0:
                first = jnp.where(dense, idx, jnp.where(above > 2, (k - above) * per, pieces))
                some_pieces(first, first + jnp.where(dense, 1, per))

        def high(x, inner):
            inside = x == 0
            attend_high(jnp.where(inside, o, o + 1 + turn // 2), jnp.where(inside, 1, turn % 2))
            return inner

        turn = idx - 1
        inner = (turn >= 0) & (turn < above - 1)
        lax.fori_loop(jnp.where((idx == 0) & (above > 0), 0, 1), jnp.where(inner, 2, 1), high, 0)
        return carry

    lax.fori_loop(2, jnp.maximum(above, 1) + 2, high_step, 0)
    def near_sums(b):
        for p in range(parts):
            x = n_far + p
            mate_copy(b, x).wait_recv()
            near_ref[b * half:(b + 1) * half, p * chunk:(p + 1) * chunk] = own_s[b, x] + mate_in[b, x].astype(F32)

    near_sums(0)
    attend_last()
    lax.fori_loop(pieces + 1, 2 * pieces, next_piece, 0)
    near_sums(1)


    for b in range(2):
        for x in range(pieces):
            mate_copy(b, x).wait_send()

    own_low(finish)
    own_high(finish)
    down(o, 1, finish)

    def drain_low(jo, carry):
        up(jo, finish)
        across(jo, 0, finish)
        return carry

    lax.fori_loop(0, o, drain_low, 0)

    def drain_above(jo, carry):
        for e in range(2):
            down(jo, e, finish)
            across(jo, e, finish)
        return carry

    lax.fori_loop(o + 1, m, drain_above, 0)

    for b in range(2):
        for x in range(n_far):
            far_copy(b, x).wait_send()
    for b in range(2):
        for x in range(n_far):
            far_copy(b, x).wait_recv()


def solution(mesh):
    n, t = mesh.shape["ctx"], mesh.shape["tp"]

    def on_device(queries, keys, values, lengths, out_weight):
        rows, width = queries.shape
        half = rows // 2
        kvw = keys.shape[1]
        kvl = kvw // HD
        group = QH // KVH
        heads = width // HD
        feat = out_weight.shape[1] // t
        chunk = min(feat, 512)
        pieces = (t // 2) * (feat // chunk)
        far = max(1, (t // 2 - 1) * (feat // chunk))
        cuts = kvl
        dma = pltpu.SemaphoreType.DMA
        hbm = pl.BlockSpec(memory_space=pl.ANY)
        near, others = pl.pallas_call(
            functools.partial(kernel, n, t, chunk),
            out_shape=[
                pltpu.VMEM((rows, feat), F32),
                pltpu.VMEM((max(1, t // 2 - 1), rows, feat), BF16),
            ],
            in_specs=[pl.BlockSpec(memory_space=pltpu.SMEM), hbm, hbm, hbm, hbm],
            out_specs=[pl.BlockSpec(memory_space=pltpu.VMEM)] * 2,
            scratch_shapes=[
                pltpu.VMEM((2, kvl, group * half, HD), BF16),
                pltpu.VMEM((n // 2, 2, 2 * half, 2 * kvw), BF16),
                pltpu.VMEM(out_weight.shape, BF16),
                pltpu.VMEM((2, kvl, group * half, half), F32),
                pltpu.VMEM((2, kvl, group * half, half), F32),
                pltpu.VMEM((2, kvl, group * half, HD), F32),
                pltpu.VMEM((half, width), BF16),
                pltpu.VMEM((2, pieces, half, chunk), F32),
                pltpu.VMEM((3, half, chunk), F32),
                pltpu.VMEM((2, pieces, half, chunk), BF16),
                pltpu.VMEM((2, pieces, half, chunk), BF16),
                pltpu.VMEM((2, far, half, chunk), BF16),
                dma((heads, 2)),
                dma((2, 2, kvl)),
                dma,
                dma((3, n // 2, 2, cuts)),
                dma((n, 2, cuts)),
                dma((2, pieces)),
                dma((2, pieces)),
                dma((2, far)),
                dma((2, far)),
            ],
            compiler_params=pltpu.CompilerParams(
                collective_id=0, has_side_effects=True, vmem_limit_bytes=56 * 1024 * 1024
            ),
        )(lengths, queries, keys, values, out_weight)
        return (near + jnp.sum(others.astype(F32), axis=0)).astype(BF16)

    return jax.shard_map(
        on_device,
        mesh=mesh,
        in_specs=(P("ctx", "tp"), P("ctx", "tp"), P("ctx", "tp"), P(), P("tp", None)),
        out_specs=P("ctx", "tp"),
        check_vma=False,
    )
```
